512 devices in a mesh: expert: 32 (over y, z_hi), dp: 16 (over x, z_lo, core).
Axes of the slice: x: 4, y: 8, z: 8 (z_hi: 4, z_lo: 2; z = z_hi * 2 + z_lo), core: 2. Of those that a mesh axis runs over, the one named last changes fastest.
Arguments:
- tokens: bfloat16 [65536, 1024], P(('expert', 'dp')), may hold values from -6 to 6
- out_grad: bfloat16 [65536, 1024], P(('expert', 'dp')), may hold values from -6 to 6
- expert_ids: int32 [65536, 8], P(('expert', 'dp')), may hold values from 0 to 127, as said below
- gate_scores: int32 [65536, 8], P(('expert', 'dp')), may hold values from 1 to 16
- w_gate: bfloat16 [512, 256, 384], P(('expert', 'dp')), may hold values from -0.1875 to 0.1875
- w_up: bfloat16 [512, 256, 384], P(('expert', 'dp')), may hold values from -0.1875 to 0.1875
- w_down: bfloat16 [512, 256, 384], P(('expert', 'dp')), may hold values from -0.3125 to 0.3125
Outputs:
- d_tokens: bfloat16 [65536, 1024], P(('expert', 'dp'))
- grad_gate: float32 [512, 256, 384], P(('expert', 'dp'))
- grad_up: float32 [512, 256, 384], P(('expert', 'dp'))
- grad_down: float32 [512, 256, 384], P(('expert', 'dp'))
The draws below stay inside these ranges and needn't reach their ends.
Inputs may be any that keep to these rules, and one draw needn't show every extreme that they name: `expert_ids`: each token names 8 different experts. Among one device's 128 tokens every expert is named by exactly 8 of them.
All inputs are finite; a program needn't handle non-finite values.
Results may differ from the reference program's by a relative error of at most 0.007.
Values may be sent and summed in bfloat16 or wider, within the bound.
A program may use at most 64 MiB of HBM per device.

```python
import jax
import jax.numpy as jnp
from jax import lax

D = 1024
HID = 384
TOP = 8
TOK_DEV = 128
EXPERTS = 128
TOKENS = 65536
DQ = 256
MOST = 8
N_EXPERT = 32
N_DP = 16


def permute_rows(row_key):
    return jax.random.permutation(row_key, TOK_DEV).astype(jnp.int32)


def permute_columns(column_key):
    return jax.random.permutation(column_key, TOP).astype(jnp.int32)


def one_block(block_key):
    key_sigma, key_rows, key_cols = jax.random.split(block_key, 3)
    sigma = jax.random.permutation(key_sigma, EXPERTS).astype(jnp.int32)
    row_orders = jax.vmap(permute_rows)(jax.random.split(key_rows, TOP))
    classes = EXPERTS // TOP
    column_index = jnp.arange(TOP, dtype=jnp.int32)
    slot_index = row_orders.T % classes * TOP + column_index[None, :]
    chosen = sigma[slot_index]
    column_orders = jax.vmap(permute_columns)(jax.random.split(key_cols, TOK_DEV))
    return jnp.take_along_axis(chosen, column_orders, axis=1)


def draw_expert_ids(key, part):
    block_total = TOKENS // TOK_DEV
    block_keys = jax.random.split(jax.random.fold_in(key, 7), block_total)
    return jax.vmap(one_block)(block_keys).reshape(TOKENS, TOP).astype(jnp.int32)


def touch_ends(result, own_key, low, largest):
    index_at = [jax.random.randint(jax.random.fold_in(own_key, axis), (), 0, length) for axis, length in enumerate(result.shape)]
    widest = result.shape.index(max(result.shape))
    neighbour = index_at[:widest] + [(index_at[widest] + 1) % result.shape[widest]] + index_at[widest + 1:]
    return result.at[tuple(index_at)].set(low).at[tuple(neighbour)].set(largest)


def level_of(stream_key, extent, cuts, low, largest):
    level, own = 1.0, jax.random.fold_in(stream_key, 6)
    for position, parts in cuts:
        draws = jnp.exp(jax.random.uniform(jax.random.fold_in(own, position), (parts,), jnp.float32, low / len(cuts), largest / len(cuts)))
        level = level * jnp.repeat(draws, extent[position] // parts).reshape([-1 if axis == position else 1 for axis in range(len(extent))])
    return level


def noise(rng, extent, width, most, cuts=(), kind=jnp.bfloat16):
    values = width * jax.random.normal(rng, extent, jnp.float32)
    if cuts:
        values = values * level_of(rng, extent, cuts, -0.22, 0.18)
    return jnp.clip(values, -most, most).astype(kind)


def setup_inputs(seed: int = 0) -> dict:
    seeds = jax.random.split(jax.random.key(seed), 8)
    return {
        "tokens": noise(seeds[0], (TOKENS, D), 1.0, 6.0, ((0, 512),)),
        "out_grad": noise(seeds[1], (TOKENS, D), 1.0, 6.0, ((0, 512),)),
        "expert_ids": draw_expert_ids(jax.random.fold_in(seeds[7], 71), 0),
        "gate_scores": touch_ends(jax.random.randint(seeds[3], (TOKENS, TOP), 1, 17), jax.random.fold_in(seeds[3], 1), 1, 16).astype(jnp.int32),
        "w_gate": noise(seeds[4], (EXPERTS * 4, DQ, HID), D ** -0.5, 0.1875, ((0, 512),)),
        "w_up": noise(seeds[5], (EXPERTS * 4, DQ, HID), D ** -0.5, 0.1875, ((0, 512),)),
        "w_down": noise(seeds[6], (EXPERTS * 4, DQ, HID), HID ** -0.5, 0.3125, ((0, 512),)),
    }


def expert_pass(rows_in, grads_in, gates_in, gate_full, up_full, down_full):
    gate_pre = jnp.dot(rows_in, gate_full, preferred_element_type=jnp.float32)
    up_pre = jnp.dot(rows_in, up_full, preferred_element_type=jnp.float32)
    sigmoid_gate = jax.nn.sigmoid(gate_pre)
    silu_gate = gate_pre * sigmoid_gate
    hidden = (silu_gate * up_pre).astype(jnp.bfloat16)
    scaled = (gates_in.astype(jnp.float32)[:, None] * grads_in.astype(jnp.float32)).astype(jnp.bfloat16)
    grad_down = jnp.dot(scaled.T, hidden, preferred_element_type=jnp.float32)
    back_hidden = jnp.dot(scaled, down_full, preferred_element_type=jnp.float32)
    gate_back = (back_hidden * up_pre * sigmoid_gate * (1.0 + gate_pre * (1.0 - sigmoid_gate))).astype(jnp.bfloat16)
    up_back = (back_hidden * silu_gate).astype(jnp.bfloat16)
    grad_gate = jnp.dot(rows_in.T, gate_back, preferred_element_type=jnp.float32)
    grad_up = jnp.dot(rows_in.T, up_back, preferred_element_type=jnp.float32)
    token_part = (jnp.dot(gate_back, gate_full.T, preferred_element_type=jnp.float32)
                  + jnp.dot(up_back, up_full.T, preferred_element_type=jnp.float32)).astype(jnp.bfloat16)
    return grad_gate, grad_up, grad_down, token_part


def reference(tokens, out_grad, expert_ids, gate_scores, w_gate, w_up, w_down):
    sources = N_EXPERT * N_DP
    routed = TOK_DEV * TOP
    source_ids = expert_ids.reshape(sources, routed)
    matches = (source_ids[:, :, None] == jnp.arange(EXPERTS, dtype=jnp.int32)[None, None, :]).astype(jnp.int32)
    before_rank = jnp.sum((jnp.cumsum(matches, axis=1) - matches) * matches, axis=2).astype(jnp.int32)
    source_index = jnp.broadcast_to(jnp.arange(sources, dtype=jnp.int32)[:, None], (sources, routed))
    row_index = jnp.arange(sources * routed, dtype=jnp.int32).reshape(sources, routed)
    padding = sources * routed
    table = jnp.full((EXPERTS, sources, MOST), padding, dtype=jnp.int32)
    table = table.at[source_ids, source_index, before_rank].set(row_index).reshape(EXPERTS, sources * MOST)
    scores = gate_scores.astype(jnp.float32)
    gate_weight = (scores / jnp.sum(scores, axis=1, keepdims=True)).astype(jnp.bfloat16)
    gate_rows = jnp.concatenate((gate_weight.reshape(-1), jnp.zeros((1,), jnp.bfloat16)))
    token_rows = jnp.concatenate((jnp.arange(padding, dtype=jnp.int32) // TOP, jnp.full((1,), TOKENS, jnp.int32)))
    token_table = jnp.concatenate((tokens, jnp.zeros((1, D), tokens.dtype)))
    grad_table = jnp.concatenate((out_grad, jnp.zeros((1, D), out_grad.dtype)))
    gate_whole = w_gate.reshape(EXPERTS, D, HID)
    up_whole = w_up.reshape(EXPERTS, D, HID)
    down_whole = w_down.reshape(EXPERTS, D, HID)

    def one_expert(accum, expert_index):
        picked = table[expert_index]
        token_index = token_rows[picked]
        grad_gate, grad_up, grad_down, token_part = expert_pass(
            token_table[token_index], grad_table[token_index], gate_rows[picked],
            gate_whole[expert_index], up_whole[expert_index], down_whole[expert_index])
        accum = accum.at[token_index].add(token_part.astype(jnp.float32))
        return accum, (grad_gate, grad_up, grad_down)

    accum, grads = lax.scan(one_expert, jnp.zeros((TOKENS + 1, D), jnp.float32), jnp.arange(EXPERTS, dtype=jnp.int32))
    layout = (EXPERTS * 4, D // 4, HID)
    return (accum[:TOKENS].astype(jnp.bfloat16), grads[0].reshape(layout),
            grads[1].reshape(layout), grads[2].reshape(layout))
```

```python
import jax
import jax.numpy as jnp
from jax import lax
from jax.experimental import pallas as pl
from jax.experimental.pallas import tpu as pltpu
from jax.sharding import PartitionSpec as P

MESH = pl.DeviceIdType.MESH
TOK = 128
D = 1024
HID = 384
EXPERTS = 128
ROWS = 1024
CHUNKS = 4
CHUNK = ROWS // CHUNKS
DQ = 256
F32 = jnp.float32
BF16 = jnp.bfloat16


def dot(lhs, rhs, contract):
    return lax.dot_general(lhs, rhs, (contract, ((), ())), preferred_element_type=F32)


def remote(src, dst, send_sem, recv_sem, device):
    return pltpu.make_async_remote_copy(
        src_ref=src, dst_ref=dst, send_sem=send_sem, recv_sem=recv_sem,
        device_id=device, device_id_type=MESH)


def device_at(x, y, z_pair, z_low, core):
    return {"expert": y * 4 + z_pair, "dp": x * 4 + z_low * 2 + core}


def dy_of(chunk, side):
    return jnp.where(side == 0, 4 - chunk, jnp.where(chunk == 0, 0, 4 + chunk))


def place_of(dy):
    return {4: (0, 0), 0: (0, 1), 3: (1, 0), 5: (1, 1), 2: (2, 0), 6: (2, 1), 1: (3, 0), 7: (3, 1)}[dy]


def slot_of(chunk, side, dx, j):
    return chunk * 32 + side * 16 + dx * 4 + j


def one_hot(condition):
    return jnp.where(condition, 1.0, 0.0)


def routing(id_blocks, expert_at, score_blocks, spread):
    each = EXPERTS // len(id_blocks)
    local = lax.broadcasted_iota(jnp.int32, (each, TOK), 0)
    experts = expert_at(local)
    members, gates = [], []
    for n, ids in enumerate(id_blocks):
        if score_blocks is not None:
            score = score_blocks[n].astype(F32)
            gate = (score / jnp.sum(score, axis=0, keepdims=True)).astype(BF16).astype(F32)
        member = jnp.zeros((each, TOK), F32)
        gate_of = jnp.zeros((each, TOK), F32)
        for k in range(8):
            hit = one_hot(experts == ids[k:k + 1, :])
            member = member + hit
            if score_blocks is not None:
                gate_of = gate_of + hit * gate[k:k + 1, :]
        members.append(member)
        gates.append(gate_of)
    member = jnp.concatenate(members, axis=0).astype(BF16)
    before = one_hot(lax.broadcasted_iota(jnp.int32, (TOK, TOK), 0)
                     < lax.broadcasted_iota(jnp.int32, (TOK, TOK), 1)).astype(BF16)
    rank = dot(member, before, ((1,), (0,)))
    wide_member = dot(spread, member, ((1,), (0,)))
    wide_rank = dot(spread, rank.astype(BF16), ((1,), (0,)))
    slot_rank = lax.rem(lax.broadcasted_iota(jnp.int32, (ROWS, TOK), 0), 8).astype(F32)
    chosen = jnp.where(wide_rank == slot_rank, wide_member, 0.0)
    if score_blocks is None:
        return chosen.astype(BF16), None
    wide_gate = dot(spread, jnp.concatenate(gates, axis=0).astype(BF16), ((1,), (0,)))
    return chosen.astype(BF16), (chosen * wide_gate).astype(BF16)


def body(tok_in, grad_in, ids_in, scores_in, wg, wu, wd, d_tok, g_gate, g_up, g_down,
         tok, grad, meta, spread, pick_y, pick_z, gated_z, ring_t, ring_i, gath_g, gath_m,
         send_t, send_g, recv_t, recv_g, part_y, part_z, ret_y, ret_z, sum_y, sum_z, got_y, got_z, weights, acc,
         half_s, half_r, quarter_s, quarter_r,
         load_sem, ring_send, ring_recv, gath_send, gath_recv, id_send, id_recv,
         send_sem, recv_t_sem, recv_g_sem, w_send, w_recv, ret_send, ret_y_sem, ret_z_sem,
         sum_send, got_y_sem, got_z_sem, red_send, red_recv):
    e_pos = lax.axis_index("expert")
    d_pos = lax.axis_index("dp")
    y, z_pair = e_pos // 4, lax.rem(e_pos, 4)
    x, part = d_pos // 4, lax.rem(d_pos, 4)
    z_low, core = part // 2, lax.rem(part, 2)
    other_core = device_at(x, y, z_pair, z_low, 1 - core)
    other_chip = device_at(x, y, z_pair, 1 - z_low, core)
    part_core = z_low * 2 + 1 - core
    part_chip = (1 - z_low) * 2 + core
    part_far = (1 - z_low) * 2 + 1 - core
    dz_near = jnp.where(z_low == 0, 1, 3)
    dz_back = 4 - dz_near
    y_next = device_at(x, lax.rem(y + 1, 8), z_pair, z_low, core)
    y_prev = device_at(x, lax.rem(y + 7, 8), z_pair, z_low, core)
    z_near = device_at(x, y, lax.rem(z_pair + dz_near, 4), z_low, core)
    z_back = device_at(x, y, lax.rem(z_pair + dz_back, 4), 1 - z_low, core)
    z_far = device_at(x, y, lax.rem(z_pair + 2, 4), 1 - z_low, core)

    def rows_of(p):
        return pl.ds(pl.multiple_of(p * DQ, DQ), DQ)

    z_from = device_at(x, y, lax.rem(z_pair + dz_back, 4), z_low, core)

    entry = pltpu.get_barrier_semaphore()

    def greet(target):
        pl.semaphore_signal(entry, inc=1, device_id=target, device_id_type=MESH)

    def greet_xy(index, carry):
        greet(device_at(lax.rem(x + lax.rem(index, 4), 4), lax.rem(y + index // 4, 8), z_pair, z_low, core))
        return carry

    def greet_xz(index, carry):
        x_to = lax.rem(x + index, 4)
        greet(device_at(x_to, y, lax.rem(z_pair + dz_near, 4), z_low, core))
        greet(device_at(x_to, y, lax.rem(z_pair + dz_back, 4), z_low, core))
        greet(device_at(x_to, y, lax.rem(z_pair + dz_back, 4), 1 - z_low, core))
        greet(device_at(x_to, y, lax.rem(z_pair + 2, 4), 1 - z_low, core))
        return carry

    greet(other_core)
    greet(other_chip)
    lax.fori_loop(0, 4, greet_xz, 0)
    lax.fori_loop(1, 32, greet_xy, 0)

    own_weights = weights.at[:, rows_of(part)]
    loads = [pltpu.make_async_copy(grad_in, grad, load_sem.at[0]),
             pltpu.make_async_copy(tok_in, tok, load_sem.at[1]),
             pltpu.make_async_copy(ids_in, meta.at[pl.ds(0, 8)], load_sem.at[2]),
             pltpu.make_async_copy(scores_in, meta.at[pl.ds(8, 8)], load_sem.at[3])]
    for i, ref in enumerate((wg, wu, wd)):
        loads.append(pltpu.make_async_copy(ref, weights.at[i, rows_of(part)], load_sem.at[4 + i]))
    for load in loads:
        load.start()
    spread[...] = one_hot(lax.broadcasted_iota(jnp.int32, (ROWS, EXPERTS), 0) // 8
                          == lax.broadcasted_iota(jnp.int32, (ROWS, EXPERTS), 1)).astype(BF16)
    acc[...] = jnp.zeros_like(acc)
    for load in loads:
        load.wait()
    pl.semaphore_wait(entry, 49)

    remote(grad, gath_g.at[2], gath_send, gath_recv.at[2], z_back).start()
    remote(grad, gath_g.at[1], gath_send, gath_recv.at[1], z_near).start()
    remote(tok, ring_t.at[1], ring_send, ring_recv.at[1], y_next).start()
    remote(tok, ring_t.at[7], ring_send, ring_recv.at[7], y_prev).start()
    for j, target in ((2, z_back), (1, z_near), (3, z_far)):
        remote(meta, gath_m.at[j], id_send.at[0], id_recv.at[0], target).start()

    def send_ids(dy, carry):
        target = device_at(x, lax.rem(y + dy, 8), z_pair, z_low, core)
        remote(meta.at[pl.ds(0, 8)], ring_i.at[dy], id_send.at[1], id_recv.at[1], target).start()
        return carry

    lax.fori_loop(1, 8, send_ids, 0)
    remote(own_weights, own_weights, w_send, w_recv.at[0], other_chip).start()
    remote(own_weights, own_weights, w_send, w_recv.at[1], other_core).start()

    def send_tokens(dy):
        block = tok if dy == 0 else ring_t.at[dy]
        chunk, side = place_of(dy)
        rows = pl.ds(dy * TOK, TOK)
        send_t[rows] = dot(pick_y[rows], block[...], ((1,), (0,))).astype(BF16)

        def one(index, carry):
            j, dx = lax.rem(index, 4), index // 4
            dz = jnp.where(j == 0, 0, jnp.where(j == 3, 2, jnp.where(j == 1, dz_near, dz_back)))
            z_low_to = jnp.where(j < 2, z_low, 1 - z_low)
            x_to, z_to = lax.rem(x + dx, 4), lax.rem(z_pair + dz, 4)
            src = pl.ds(pl.multiple_of(dy * TOK + (z_to * 4 + x_to) * 8, 8), 8)
            dst = pl.ds(pl.multiple_of(slot_of(chunk, side, dx, j) * 8, 8), 8)

            @pl.when(index == 0)
            def _():
                pltpu.make_async_copy(send_t.at[src], recv_t.at[dst], recv_t_sem.at[chunk]).start()

            @pl.when(index > 0)
            def _():
                target = device_at(x_to, y, z_to, z_low_to, core)
                remote(send_t.at[src], recv_t.at[dst], send_sem.at[0], recv_t_sem.at[chunk], target).start()

            return carry

        lax.fori_loop(0, 16, one, 0)

    def send_grads(j):
        block = grad if j == 0 else gath_g.at[j]
        rows = pl.ds(j * 256, 256)
        send_g[rows] = dot(gated_z[rows], block[...], ((1,), (0,))).astype(BF16)

        def one(index, carry):
            chunk, side, dx = index // 8, lax.rem(index, 2), lax.rem(index // 2, 4)
            dy = dy_of(chunk, side)
            x_to, y_to = lax.rem(x + dx, 4), lax.rem(y + dy, 8)
            src = pl.ds(pl.multiple_of(j * 256 + (y_to * 4 + x_to) * 8, 8), 8)
            dst = pl.ds(pl.multiple_of(slot_of(chunk, side, dx, j) * 8, 8), 8)
            here = (dx + dy) == 0

            @pl.when(here)
            def _():
                pltpu.make_async_copy(send_g.at[src], recv_g.at[dst], recv_g_sem.at[chunk]).start()

            @pl.when(jnp.logical_not(here))
            def _():
                target = device_at(x_to, y_to, z_pair, z_low, core)
                remote(send_g.at[src], recv_g.at[dst], send_sem.at[1], recv_g_sem.at[chunk], target).start()

            return carry

        lax.fori_loop(0, 32, one, 0)

    def wait_ring(dy):
        pltpu.make_async_copy(ring_t.at[dy], ring_t.at[dy], ring_recv.at[dy]).wait()

    def pass_on(dy, to, target, rows=None):
        src, dst = ring_t.at[dy], ring_t.at[to]
        if rows is not None:
            src, dst = src.at[rows], dst.at[rows]
        remote(src, dst, ring_send, ring_recv.at[to], target).start()

    def wait_gath(j):
        pltpu.make_async_copy(gath_g.at[j], gath_g.at[j], gath_recv.at[j]).wait()

    metas = gath_m.at[pl.ds(1, 3)]
    pltpu.make_async_copy(metas, metas, id_recv.at[0]).wait()
    all_ids = ring_i.at[pl.ds(1, 7)]
    pltpu.make_async_copy(all_ids, all_ids, id_recv.at[1]).wait()
    pick_z[...], gated_z[...] = routing([meta[0:8]] + [gath_m[j, 0:8] for j in range(1, 4)],
                                        lambda e: (e // 4) * 16 + z_pair * 4 + lax.rem(e, 4),
                                        [meta[8:16]] + [gath_m[j, 8:16] for j in range(1, 4)], spread[...])
    send_grads(0)
    wait_ring(1)
    pass_on(1, 2, y_next)
    wait_ring(7)
    pass_on(7, 6, y_prev)
    wait_gath(2)
    remote(gath_g.at[2], gath_g.at[3], gath_send, gath_recv.at[3], z_near).start()
    pick_y[...], _ = routing([meta[0:8]] + [ring_i[dy] for dy in range(1, 8)], lambda e: y * 16 + e, None, spread[...])
    send_grads(2)
    send_tokens(1)
    send_tokens(7)
    w_chip = weights.at[:, rows_of(part_chip)]
    pltpu.make_async_copy(w_chip, w_chip, w_recv.at[0]).wait()
    remote(w_chip, w_chip, w_send, w_recv.at[2], other_core).start()
    wait_ring(2)
    pass_on(2, 3, y_next)
    wait_ring(6)
    pass_on(6, 5, y_prev)
    wait_gath(1)
    send_grads(1)
    send_tokens(2)
    send_tokens(6)
    wait_gath(3)
    send_grads(3)
    wait_ring(3)
    pass_on(3, 4, y_next, pl.ds(0, TOK // 2))
    wait_ring(5)
    pass_on(5, 4, y_prev, pl.ds(TOK // 2, TOK // 2))
    send_tokens(3)
    send_tokens(5)
    send_tokens(0)
    wait_ring(4)
    send_tokens(4)
    w_core = weights.at[:, rows_of(part_core)]
    w_far = weights.at[:, rows_of(part_far)]
    pltpu.make_async_copy(w_core, w_core, w_recv.at[1]).wait()
    pltpu.make_async_copy(w_far, w_far, w_recv.at[2]).wait()

    def compute(c):
        rows = pl.ds(c * CHUNK, CHUNK)
        pltpu.make_async_copy(recv_t.at[rows], recv_t.at[rows], recv_t_sem.at[c]).wait()
        pltpu.make_async_copy(recv_g.at[rows], recv_g.at[rows], recv_g_sem.at[c]).wait()
        row_in = recv_t[rows]
        scaled = recv_g[rows]
        a = dot(row_in, weights[0], ((1,), (0,)))
        b = dot(row_in, weights[1], ((1,), (0,)))
        back = dot(scaled, weights[2], ((1,), (0,)))
        sig = jax.nn.sigmoid(a)
        silu = a * sig
        hidden = (silu * b).astype(BF16)
        gate_back = (back * b * sig * (1.0 + a * (1.0 - sig))).astype(BF16)
        up_back = (back * silu).astype(BF16)
        token_part = (dot(gate_back, weights[0], ((1,), (1,)))
                      + dot(up_back, weights[1], ((1,), (1,)))).astype(BF16)
        part_y[rows] = token_part[:, :D // 2]
        part_z[rows] = token_part[:, D // 2:]

        def give_back(index, carry):
            side, j, dx = lax.rem(index, 2), lax.rem(index // 2, 4), index // 8
            dy = dy_of(c, side)
            dz = jnp.where(j == 0, 0, jnp.where(j == 3, 2, dz_near))
            z_low_from = jnp.where(j < 2, z_low, 1 - z_low)
            x_to, y_to, z_to = lax.rem(x + 4 - dx, 4), lax.rem(y + 8 - dy, 8), lax.rem(z_pair + 4 - dz, 4)
            src = pl.ds(pl.multiple_of(slot_of(c, side, dx, j) * 8, 8), 8)
            dst_y = ret_y.at[dy, pl.ds(pl.multiple_of((z_pair * 4 + x) * 8, 8), 8)]
            dst_z = ret_z.at[j, pl.ds(pl.multiple_of((y * 4 + x) * 8, 8), 8)]
            stays_y = (dx + j) == 0
            stays_z = (dx + dy) == 0

            @pl.when(stays_z)
            def _():
                pltpu.make_async_copy(part_z.at[src], dst_z, ret_z_sem.at[j]).start()

            @pl.when(jnp.logical_not(stays_z))
            def _():
                target = device_at(x_to, y_to, z_pair, z_low, core)
                remote(part_z.at[src], dst_z, ret_send.at[1], ret_z_sem.at[j], target).start()

            @pl.when(stays_y)
            def _():
                pltpu.make_async_copy(part_y.at[src], dst_y, ret_y_sem.at[dy]).start()

            @pl.when(jnp.logical_not(stays_y))
            def _():
                target = device_at(x_to, y, z_to, z_low_from, core)
                remote(part_y.at[src], dst_y, ret_send.at[0], ret_y_sem.at[dy], target).start()

            return carry

        lax.fori_loop(0, 32, give_back, 0)
        acc[0] += dot(row_in, gate_back, ((0,), (0,)))
        acc[1] += dot(row_in, up_back, ((0,), (0,)))
        acc[2] += dot(scaled, hidden, ((0,), (0,)))

    def per_token_y(dy):
        pltpu.make_async_copy(ret_y.at[dy], ret_y.at[dy], ret_y_sem.at[dy]).wait()
        return dot(pick_y[pl.ds(dy * TOK, TOK)], ret_y[dy], ((0,), (0,)))

    def per_token_z(j):
        pltpu.make_async_copy(ret_z.at[j], ret_z.at[j], ret_z_sem.at[j]).wait()
        return dot(pick_z[pl.ds(j * 256, 256)], ret_z[j], ((0,), (0,)))

    low, high = pl.ds(0, TOK // 2), pl.ds(TOK // 2, TOK // 2)

    def wait_got_y(slot, rows=None):
        ref = got_y.at[slot] if rows is None else got_y.at[slot, rows]
        pltpu.make_async_copy(ref, ref, got_y_sem.at[slot]).wait()

    def start_sum_y():
        sum_y[4] = per_token_y(4).astype(BF16)
        remote(sum_y.at[4, low], got_y.at[3, low], sum_send.at[0], got_y_sem.at[3], y_prev).start()
        remote(sum_y.at[4, high], got_y.at[5, high], sum_send.at[0], got_y_sem.at[5], y_next).start()

    def step_sum_y(dy, to, target):
        total = per_token_y(dy)
        if dy == 3:
            wait_got_y(3, low)
            half = TOK // 2
            sum_y[3, 0:half] = (total[0:half] + got_y[3, 0:half].astype(F32)).astype(BF16)
            sum_y[3, half:TOK] = total[half:TOK].astype(BF16)
        elif dy == 5:
            wait_got_y(5, high)
            half = TOK // 2
            sum_y[5, 0:half] = total[0:half].astype(BF16)
            sum_y[5, half:TOK] = (total[half:TOK] + got_y[5, half:TOK].astype(F32)).astype(BF16)
        else:
            wait_got_y(dy)
            sum_y[dy] = (total + got_y[dy].astype(F32)).astype(BF16)
        remote(sum_y.at[dy], got_y.at[to], sum_send.at[0], got_y_sem.at[to], target).start()

    compute(0)
    compute(1)
    start_sum_y()
    compute(2)
    step_sum_y(3, 2, y_prev)
    step_sum_y(5, 6, y_next)
    compute(3)
    for i in range(3):
        for zl in range(2):
            half_s[i, zl] = acc[i, rows_of(zl * 2 + 1 - core)].astype(BF16)
    half = remote(half_s, half_r, red_send.at[0], red_recv.at[0], other_core)
    half.start()
    step_sum_y(2, 1, y_prev)
    step_sum_y(6, 7, y_next)
    half.wait()
    for i in range(3):
        quarter_s[i] = (acc[i, rows_of(part_chip)] + half_r[i, 1 - z_low].astype(F32)).astype(BF16)
    quarter = remote(quarter_s, quarter_r, red_send.at[1], red_recv.at[1], other_chip)
    quarter.start()
    sum_z[3] = per_token_z(3).astype(BF16)
    remote(sum_z.at[3], got_z.at[3], sum_send.at[1], got_z_sem.at[3], z_from).start()
    step_sum_y(1, 0, y_prev)
    step_sum_y(7, 4, y_next)
    sum_z[1] = per_token_z(1).astype(BF16)
    remote(sum_z.at[1], got_z.at[1], sum_send.at[1], got_z_sem.at[1], z_from).start()
    own_z2 = per_token_z(2)
    pltpu.make_async_copy(got_z.at[3], got_z.at[3], got_z_sem.at[3]).wait()
    sum_z[2] = (own_z2 + got_z[3].astype(F32)).astype(BF16)
    remote(sum_z.at[2], got_z.at[2], sum_send.at[1], got_z_sem.at[2], z_back).start()
    own_y = per_token_y(0)
    own_z = per_token_z(0)
    wait_got_y(0)
    wait_got_y(4)
    d_tok[:, 0:D // 2] = (own_y + got_y[0].astype(F32) + got_y[4].astype(F32)).astype(BF16)
    quarter.wait()
    outs = (g_gate, g_up, g_down)
    for i in range(3):
        outs[i][...] = acc[i, rows_of(part)] + half_r[i, z_low].astype(F32) + quarter_r[i].astype(F32)
    pltpu.make_async_copy(got_z.at[1], got_z.at[1], got_z_sem.at[1]).wait()
    pltpu.make_async_copy(got_z.at[2], got_z.at[2], got_z_sem.at[2]).wait()
    d_tok[:, D // 2:D] = (own_z + got_z[1].astype(F32) + got_z[2].astype(F32)).astype(BF16)

    def wait_sent(ref, sem):
        pltpu.make_async_copy(ref, ref, sem).wait()

    wait_sent(send_t.at[pl.ds(0, ROWS - 64)], send_sem.at[0])
    wait_sent(send_g.at[pl.ds(0, ROWS - 32)], send_sem.at[1])
    wait_sent(part_y.at[pl.ds(0, ROWS - 64)], ret_send.at[0])
    wait_sent(part_z.at[pl.ds(0, ROWS - 32)], ret_send.at[1])
    wait_sent(ring_t.at[pl.ds(1, 7)], ring_send)
    wait_sent(gath_g.at[pl.ds(1, 3)], gath_send)
    wait_sent(metas, id_send.at[0])
    wait_sent(all_ids, id_send.at[1])
    wait_sent(sum_y.at[pl.ds(1, 7)], sum_send.at[0])
    wait_sent(sum_z.at[pl.ds(1, 3)], sum_send.at[1])
    for _ in range(3):
        wait_sent(w_chip, w_send)


def per_device(tokens, out_grad, expert_ids, gate_scores, w_gate, w_up, w_down):
    vmem = pl.BlockSpec(memory_space=pltpu.VMEM)
    block = jax.ShapeDtypeStruct((DQ, HID), F32)
    dma = pltpu.SemaphoreType.DMA
    half = D // 2
    d_tokens, gate, up, down = pl.pallas_call(
        body,
        out_shape=(jax.ShapeDtypeStruct((TOK, D), BF16), block, block, block),
        in_specs=[pl.BlockSpec(memory_space=pl.ANY)] * 7,
        out_specs=(vmem,) * 4,
        scratch_shapes=[
            pltpu.VMEM((TOK, D), BF16),
            pltpu.VMEM((TOK, D), BF16),
            pltpu.VMEM((16, TOK), jnp.int32),
            pltpu.VMEM((ROWS, EXPERTS), BF16),
            pltpu.VMEM((ROWS, TOK), BF16),
            pltpu.VMEM((ROWS, TOK), BF16),
            pltpu.VMEM((ROWS, TOK), BF16),
            pltpu.VMEM((8, TOK, D), BF16),
            pltpu.VMEM((8, 8, TOK), jnp.int32),
            pltpu.VMEM((4, TOK, D), BF16),
            pltpu.VMEM((4, 16, TOK), jnp.int32),
            pltpu.VMEM((ROWS, D), BF16),
            pltpu.VMEM((ROWS, D), BF16),
            pltpu.VMEM((ROWS, D), BF16),
            pltpu.VMEM((ROWS, D), BF16),
            pltpu.VMEM((ROWS, half), BF16),
            pltpu.VMEM((ROWS, half), BF16),
            pltpu.VMEM((8, TOK, half), BF16),
            pltpu.VMEM((4, 256, half), BF16),
            pltpu.VMEM((8, TOK, half), BF16),
            pltpu.VMEM((4, TOK, half), BF16),
            pltpu.VMEM((8, TOK, half), BF16),
            pltpu.VMEM((4, TOK, half), BF16),
            pltpu.VMEM((3, D, HID), BF16),
            pltpu.VMEM((3, D, HID), F32),
            pltpu.VMEM((3, 2, DQ, HID), BF16),
            pltpu.VMEM((3, 2, DQ, HID), BF16),
            pltpu.VMEM((3, DQ, HID), BF16),
            pltpu.VMEM((3, DQ, HID), BF16),
            dma((7,)),
            dma,
            dma((8,)),
            dma,
            dma((4,)),
            dma((2,)),
            dma((2,)),
            dma((2,)),
            dma((CHUNKS,)),
            dma((CHUNKS,)),
            dma,
            dma((3,)),
            dma((2,)),
            dma((8,)),
            dma((4,)),
            dma((2,)),
            dma((8,)),
            dma((4,)),
            dma((2,)),
            dma((2,)),
        ],
        compiler_params=pltpu.CompilerParams(
            collective_id=0, has_side_effects=True, vmem_limit_bytes=56 << 20),
        name="expert_layer_backward",
    )(tokens, out_grad, expert_ids.T, gate_scores.T, w_gate[0], w_up[0], w_down[0])
    return d_tokens, gate[None], up[None], down[None]


def solution(mesh):
    rows = P(("expert", "dp"), None)
    blocks = P(("expert", "dp"), None, None)
    return jax.shard_map(
        per_device,
        mesh=mesh,
        in_specs=(rows, rows, rows, rows, blocks, blocks, blocks),
        out_specs=(rows, blocks, blocks, blocks),
        check_vma=False,
    )
```

```python
import jax
import jax.numpy as jnp
from jax import lax
from jax.experimental import pallas as pl
from jax.experimental.pallas import tpu as pltpu
from jax.sharding import PartitionSpec as P

MESH = pl.DeviceIdType.MESH
TOK = 128
D = 1024
HID = 384
EXPERTS = 128
ROWS = 1024
CHUNKS = 4
SUB = 2
CHUNK = ROWS // CHUNKS
DQ = 256
F32 = jnp.float32
BF16 = jnp.bfloat16


def dot(lhs, rhs, contract):
    return lax.dot_general(lhs, rhs, (contract, ((), ())), preferred_element_type=F32)


def remote(src, dst, send_sem, recv_sem, device):
    return pltpu.make_async_remote_copy(
        src_ref=src, dst_ref=dst, send_sem=send_sem, recv_sem=recv_sem,
        device_id=device, device_id_type=MESH)


def device_at(x, y, z_pair, z_low, core):
    return {"expert": y * 4 + z_pair, "dp": x * 4 + z_low * 2 + core}


def dy_of(chunk, side):
    return jnp.where(side == 0, 4 - chunk, jnp.where(chunk == 0, 0, 4 + chunk))


def place_of(dy):
    return {4: (0, 0), 0: (0, 1), 3: (1, 0), 5: (1, 1), 2: (2, 0), 6: (2, 1), 1: (3, 0), 7: (3, 1)}[dy]


def slot_of(chunk, side, dx, j):
    return chunk * 32 + side * 16 + dx * 4 + j


def one_hot(condition):
    return jnp.where(condition, 1.0, 0.0)


def routing(id_blocks, expert_at, score_blocks, spread):
    each = EXPERTS // len(id_blocks)
    local = lax.broadcasted_iota(jnp.int32, (each, TOK), 0)
    experts = expert_at(local)
    members, gates = [], []
    for n, ids in enumerate(id_blocks):
        if score_blocks is not None:
            score = score_blocks[n].astype(F32)
            gate = (score / jnp.sum(score, axis=0, keepdims=True)).astype(BF16).astype(F32)
        member = jnp.zeros((each, TOK), F32)
        gate_of = jnp.zeros((each, TOK), F32)
        for k in range(8):
            hit = one_hot(experts == ids[k:k + 1, :])
            member = member + hit
            if score_blocks is not None:
                gate_of = gate_of + hit * gate[k:k + 1, :]
        members.append(member)
        gates.append(gate_of)
    member = jnp.concatenate(members, axis=0).astype(BF16)
    before = one_hot(lax.broadcasted_iota(jnp.int32, (TOK, TOK), 0)
                     < lax.broadcasted_iota(jnp.int32, (TOK, TOK), 1)).astype(BF16)
    rank = dot(member, before, ((1,), (0,)))
    wide_member = dot(spread, member, ((1,), (0,)))
    wide_rank = dot(spread, rank.astype(BF16), ((1,), (0,)))
    slot_rank = lax.rem(lax.broadcasted_iota(jnp.int32, (ROWS, TOK), 0), 8).astype(F32)
    chosen = jnp.where(wide_rank == slot_rank, wide_member, 0.0)
    if score_blocks is None:
        return chosen.astype(BF16), None
    wide_gate = dot(spread, jnp.concatenate(gates, axis=0).astype(BF16), ((1,), (0,)))
    return chosen.astype(BF16), (chosen * wide_gate).astype(BF16)


def body(tok_in, grad_in, ids_in, scores_in, wg, wu, wd, d_tok, g_gate, g_up, g_down,
         tok, grad, meta, spread, pick_y, pick_z, gated_z, ring_t, ring_i, gath_g, gath_m,
         send_t, send_g, recv_t, recv_g, part_y, part_z, ret_y, ret_z, sum_y, sum_z, got_y, got_z, weights, acc,
         half_s, half_r, quarter_s, quarter_r,
         load_sem, ring_send, ring_recv, gath_send, gath_recv, id_send, id_recv,
         send_sem, recv_t_sem, recv_g_sem, w_send, w_recv, ret_send, ret_y_sem, ret_z_sem,
         sum_send, got_y_sem, got_z_sem, red_send, red_recv):
    e_pos = lax.axis_index("expert")
    d_pos = lax.axis_index("dp")
    y, z_pair = e_pos // 4, lax.rem(e_pos, 4)
    x, part = d_pos // 4, lax.rem(d_pos, 4)
    z_low, core = part // 2, lax.rem(part, 2)
    other_core = device_at(x, y, z_pair, z_low, 1 - core)
    other_chip = device_at(x, y, z_pair, 1 - z_low, core)
    part_core = z_low * 2 + 1 - core
    part_chip = (1 - z_low) * 2 + core
    part_far = (1 - z_low) * 2 + 1 - core
    dz_near = jnp.where(z_low == 0, 1, 3)
    dz_back = 4 - dz_near
    y_next = device_at(x, lax.rem(y + 1, 8), z_pair, z_low, core)
    y_prev = device_at(x, lax.rem(y + 7, 8), z_pair, z_low, core)
    z_near = device_at(x, y, lax.rem(z_pair + dz_near, 4), z_low, core)
    z_back = device_at(x, y, lax.rem(z_pair + dz_back, 4), 1 - z_low, core)
    z_far = device_at(x, y, lax.rem(z_pair + 2, 4), 1 - z_low, core)

    def rows_of(p):
        return pl.ds(pl.multiple_of(p * DQ, DQ), DQ)

    z_from = device_at(x, y, lax.rem(z_pair + dz_back, 4), z_low, core)

    entry = pltpu.get_barrier_semaphore()

    def greet(target):
        pl.semaphore_signal(entry, inc=1, device_id=target, device_id_type=MESH)

    def greet_xy(index, carry):
        greet(device_at(lax.rem(x + lax.rem(index, 4), 4), lax.rem(y + index // 4, 8), z_pair, z_low, core))
        return carry

    def greet_xz(index, carry):
        x_to = lax.rem(x + index, 4)
        greet(device_at(x_to, y, lax.rem(z_pair + dz_near, 4), z_low, core))
        greet(device_at(x_to, y, lax.rem(z_pair + dz_back, 4), z_low, core))
        greet(device_at(x_to, y, lax.rem(z_pair + dz_back, 4), 1 - z_low, core))
        greet(device_at(x_to, y, lax.rem(z_pair + 2, 4), 1 - z_low, core))
        return carry

    greet(other_core)
    greet(other_chip)
    lax.fori_loop(0, 4, greet_xz, 0)
    lax.fori_loop(1, 32, greet_xy, 0)

    own_weights = weights.at[:, rows_of(part)]
    loads = [pltpu.make_async_copy(grad_in, grad, load_sem.at[0]),
             pltpu.make_async_copy(tok_in, tok, load_sem.at[1]),
             pltpu.make_async_copy(ids_in, meta.at[pl.ds(0, 8)], load_sem.at[2]),
             pltpu.make_async_copy(scores_in, meta.at[pl.ds(8, 8)], load_sem.at[3])]
    for i, ref in enumerate((wg, wu, wd)):
        loads.append(pltpu.make_async_copy(ref, weights.at[i, rows_of(part)], load_sem.at[4 + i]))
    for load in loads:
        load.start()
    spread[...] = one_hot(lax.broadcasted_iota(jnp.int32, (ROWS, EXPERTS), 0) // 8
                          == lax.broadcasted_iota(jnp.int32, (ROWS, EXPERTS), 1)).astype(BF16)
    acc[...] = jnp.zeros_like(acc)
    for load in loads:
        load.wait()
    pl.semaphore_wait(entry, 49)

    remote(grad, gath_g.at[2], gath_send, gath_recv.at[2], z_back).start()
    remote(grad, gath_g.at[1], gath_send, gath_recv.at[1], z_near).start()
    for n in range(SUB):
        rows = pl.ds(n * (TOK // SUB), TOK // SUB)
        remote(tok.at[rows], ring_t.at[1, rows], ring_send, ring_recv.at[1, n], y_next).start()
        remote(tok.at[rows], ring_t.at[7, rows], ring_send, ring_recv.at[7, n], y_prev).start()
    for j, target in ((2, z_back), (1, z_near), (3, z_far)):
        remote(meta, gath_m.at[j], id_send.at[0], id_recv.at[0], target).start()

    def send_ids(dy, carry):
        target = device_at(x, lax.rem(y + dy, 8), z_pair, z_low, core)
        remote(meta.at[pl.ds(0, 8)], ring_i.at[dy], id_send.at[1], id_recv.at[1], target).start()
        return carry

    lax.fori_loop(1, 8, send_ids, 0)
    remote(own_weights, own_weights, w_send, w_recv.at[0], other_chip).start()
    remote(own_weights, own_weights, w_send, w_recv.at[1], other_core).start()

    def send_tokens(dy):
        block = tok if dy == 0 else ring_t.at[dy]
        chunk, side = place_of(dy)
        rows = pl.ds(dy * TOK, TOK)
        send_t[rows] = dot(pick_y[rows], block[...], ((1,), (0,))).astype(BF16)

        def one(index, carry):
            j, dx = lax.rem(index, 4), index // 4
            dz = jnp.where(j == 0, 0, jnp.where(j == 3, 2, jnp.where(j == 1, dz_near, dz_back)))
            z_low_to = jnp.where(j < 2, z_low, 1 - z_low)
            x_to, z_to = lax.rem(x + dx, 4), lax.rem(z_pair + dz, 4)
            src = pl.ds(pl.multiple_of(dy * TOK + (z_to * 4 + x_to) * 8, 8), 8)
            dst = pl.ds(pl.multiple_of(slot_of(chunk, side, dx, j) * 8, 8), 8)

            @pl.when(index == 0)
            def _():
                pltpu.make_async_copy(send_t.at[src], recv_t.at[dst], recv_t_sem.at[chunk]).start()

            @pl.when(index > 0)
            def _():
                target = device_at(x_to, y, z_to, z_low_to, core)
                remote(send_t.at[src], recv_t.at[dst], send_sem.at[0], recv_t_sem.at[chunk], target).start()

            return carry

        lax.fori_loop(0, 16, one, 0)

    def scale_grads(j):
        block = grad if j == 0 else gath_g.at[j]
        rows = pl.ds(j * 256, 256)
        send_g[rows] = dot(gated_z[rows], block[...], ((1,), (0,))).astype(BF16)

    def send_grads(chunk):
        def one(index, carry):
            side, j, dx = lax.rem(index, 2), lax.rem(index // 2, 4), index // 8
            dy = dy_of(chunk, side)
            x_to, y_to = lax.rem(x + dx, 4), lax.rem(y + dy, 8)
            src = pl.ds(pl.multiple_of(j * 256 + (y_to * 4 + x_to) * 8, 8), 8)
            dst = pl.ds(pl.multiple_of(slot_of(chunk, side, dx, j) * 8, 8), 8)
            here = (dx + dy) == 0

            @pl.when(here)
            def _():
                pltpu.make_async_copy(send_g.at[src], recv_g.at[dst], recv_g_sem.at[chunk]).start()

            @pl.when(jnp.logical_not(here))
            def _():
                target = device_at(x_to, y_to, z_pair, z_low, core)
                remote(send_g.at[src], recv_g.at[dst], send_sem.at[1], recv_g_sem.at[chunk], target).start()

            return carry

        lax.fori_loop(0, 32, one, 0)

    def ring_rows(n):
        return pl.ds(n * (TOK // SUB), TOK // SUB)

    def wait_ring(dy, n):
        ref = ring_t.at[dy, ring_rows(n)]
        pltpu.make_async_copy(ref, ref, ring_recv.at[dy, n]).wait()

    def pass_on(dy, to, n, target):
        remote(ring_t.at[dy, ring_rows(n)], ring_t.at[to, ring_rows(n)],
               ring_send, ring_recv.at[to, n], target).start()

    def wait_gath(j):
        pltpu.make_async_copy(gath_g.at[j], gath_g.at[j], gath_recv.at[j]).wait()

    metas = gath_m.at[pl.ds(1, 3)]
    pltpu.make_async_copy(metas, metas, id_recv.at[0]).wait()
    all_ids = ring_i.at[pl.ds(1, 7)]
    pltpu.make_async_copy(all_ids, all_ids, id_recv.at[1]).wait()
    pick_z[...], gated_z[...] = routing([meta[0:8]] + [gath_m[j, 0:8] for j in range(1, 4)],
                                        lambda e: (e // 4) * 16 + z_pair * 4 + lax.rem(e, 4),
                                        [meta[8:16]] + [gath_m[j, 8:16] for j in range(1, 4)], spread[...])
    def make_pick_y():
        pick_y[...], _ = routing([meta[0:8]] + [ring_i[dy] for dy in range(1, 8)], lambda e: y * 16 + e, None, spread[...])

    def hops(step):
        for n in range(SUB):
            wait_ring(step, n)
            if step < 3 or n < SUB // 2:
                pass_on(step, step + 1, n, y_next)
            wait_ring(8 - step, n)
            if step < 3 or n >= SUB // 2:
                pass_on(8 - step, 7 - step, n, y_prev)

    def relay():
        wait_gath(2)
        remote(gath_g.at[2], gath_g.at[3], gath_send, gath_recv.at[3], z_near).start()

    w_chip = weights.at[:, rows_of(part_chip)]

    def pass_weights():
        pltpu.make_async_copy(w_chip, w_chip, w_recv.at[0]).wait()
        remote(w_chip, w_chip, w_send, w_recv.at[2], other_core).start()

    def last_block():
        for n in range(SUB):
            wait_ring(4, n)

    def wait_weights():
        for n, p in ((1, part_core), (2, part_far)):
            ref = weights.at[:, rows_of(p)]
            pltpu.make_async_copy(ref, ref, w_recv.at[n]).wait()

    def compute(c):
        rows = pl.ds(c * CHUNK, CHUNK)
        pltpu.make_async_copy(recv_t.at[rows], recv_t.at[rows], recv_t_sem.at[c]).wait()
        pltpu.make_async_copy(recv_g.at[rows], recv_g.at[rows], recv_g_sem.at[c]).wait()
        row_in = recv_t[rows]
        scaled = recv_g[rows]
        a = dot(row_in, weights[0], ((1,), (0,)))
        b = dot(row_in, weights[1], ((1,), (0,)))
        back = dot(scaled, weights[2], ((1,), (0,)))
        sig = jax.nn.sigmoid(a)
        silu = a * sig
        hidden = (silu * b).astype(BF16)
        gate_back = (back * b * sig * (1.0 + a * (1.0 - sig))).astype(BF16)
        up_back = (back * silu).astype(BF16)
        token_part = (dot(gate_back, weights[0], ((1,), (1,)))
                      + dot(up_back, weights[1], ((1,), (1,)))).astype(BF16)
        part_y[rows] = token_part[:, :D // 2]
        part_z[rows] = token_part[:, D // 2:]

        def give_back(index, carry):
            side, j, dx = lax.rem(index, 2), lax.rem(index // 2, 4), index // 8
            dy = dy_of(c, side)
            dz = jnp.where(j == 0, 0, jnp.where(j == 3, 2, dz_near))
            z_low_from = jnp.where(j < 2, z_low, 1 - z_low)
            x_to, y_to, z_to = lax.rem(x + 4 - dx, 4), lax.rem(y + 8 - dy, 8), lax.rem(z_pair + 4 - dz, 4)
            src = pl.ds(pl.multiple_of(slot_of(c, side, dx, j) * 8, 8), 8)
            dst_y = ret_y.at[dy, pl.ds(pl.multiple_of((z_pair * 4 + x) * 8, 8), 8)]
            dst_z = ret_z.at[j, pl.ds(pl.multiple_of((y * 4 + x) * 8, 8), 8)]
            stays_y = (dx + j) == 0
            stays_z = (dx + dy) == 0

            @pl.when(stays_z)
            def _():
                pltpu.make_async_copy(part_z.at[src], dst_z, ret_z_sem.at[j]).start()

            @pl.when(jnp.logical_not(stays_z))
            def _():
                target = device_at(x_to, y_to, z_pair, z_low, core)
                remote(part_z.at[src], dst_z, ret_send.at[1], ret_z_sem.at[j], target).start()

            @pl.when(stays_y)
            def _():
                pltpu.make_async_copy(part_y.at[src], dst_y, ret_y_sem.at[dy]).start()

            @pl.when(jnp.logical_not(stays_y))
            def _():
                target = device_at(x_to, y, z_to, z_low_from, core)
                remote(part_y.at[src], dst_y, ret_send.at[0], ret_y_sem.at[dy], target).start()

            return carry

        lax.fori_loop(0, 32, give_back, 0)
        acc[0] += dot(row_in, gate_back, ((0,), (0,)))
        acc[1] += dot(row_in, up_back, ((0,), (0,)))
        if c == CHUNKS - 1:
            start_half(0)
            start_half(1)
        acc[2] += dot(scaled, hidden, ((0,), (0,)))
        if c == CHUNKS - 1:
            start_half(2)

    def per_token_y(dy):
        pltpu.make_async_copy(ret_y.at[dy], ret_y.at[dy], ret_y_sem.at[dy]).wait()
        return dot(pick_y[pl.ds(dy * TOK, TOK)], ret_y[dy], ((0,), (0,)))

    def per_token_z(j):
        pltpu.make_async_copy(ret_z.at[j], ret_z.at[j], ret_z_sem.at[j]).wait()
        return dot(pick_z[pl.ds(j * 256, 256)], ret_z[j], ((0,), (0,)))

    low, high = pl.ds(0, TOK // 2), pl.ds(TOK // 2, TOK // 2)

    def wait_got_y(slot, rows=None):
        ref = got_y.at[slot] if rows is None else got_y.at[slot, rows]
        pltpu.make_async_copy(ref, ref, got_y_sem.at[slot]).wait()

    def start_sum_y():
        sum_y[4] = per_token_y(4).astype(BF16)
        remote(sum_y.at[4, low], got_y.at[3, low], sum_send.at[0], got_y_sem.at[3], y_prev).start()
        remote(sum_y.at[4, high], got_y.at[5, high], sum_send.at[0], got_y_sem.at[5], y_next).start()

    def step_sum_y(dy, to, target):
        total = per_token_y(dy)
        if dy == 3:
            wait_got_y(3, low)
            half = TOK // 2
            sum_y[3, 0:half] = (total[0:half] + got_y[3, 0:half].astype(F32)).astype(BF16)
            sum_y[3, half:TOK] = total[half:TOK].astype(BF16)
        elif dy == 5:
            wait_got_y(5, high)
            half = TOK // 2
            sum_y[5, 0:half] = total[0:half].astype(BF16)
            sum_y[5, half:TOK] = (total[half:TOK] + got_y[5, half:TOK].astype(F32)).astype(BF16)
        else:
            wait_got_y(dy)
            sum_y[dy] = (total + got_y[dy].astype(F32)).astype(BF16)
        remote(sum_y.at[dy], got_y.at[to], sum_send.at[0], got_y_sem.at[to], target).start()

    def half(i):
        return remote(half_s.at[i], half_r.at[i], red_send.at[i], red_recv.at[i], other_core)

    def quarter(i):
        return remote(quarter_s.at[i], quarter_r.at[i], red_send.at[3 + i], red_recv.at[3 + i], other_chip)

    def start_half(i):
        for zl in range(2):
            half_s[i, zl] = acc[i, rows_of(zl * 2 + 1 - core)].astype(BF16)
        half(i).start()

    def wait_half(i):
        half(i).wait()

    hops(1)
    relay()
    make_pick_y()
    send_tokens(0)
    scale_grads(0)
    hops(2)
    scale_grads(2)
    send_tokens(1)
    send_tokens(7)
    pass_weights()
    wait_gath(1)
    scale_grads(1)
    hops(3)
    wait_gath(3)
    scale_grads(3)
    send_grads(0)
    send_tokens(3)
    send_tokens(5)
    last_block()
    send_tokens(4)
    send_grads(1)
    send_tokens(2)
    send_tokens(6)
    send_grads(2)
    wait_weights()
    compute(0)
    send_grads(3)
    compute(1)
    start_sum_y()
    compute(2)
    step_sum_y(3, 2, y_prev)
    step_sum_y(5, 6, y_next)
    compute(3)
    step_sum_y(2, 1, y_prev)
    step_sum_y(6, 7, y_next)
    for i in range(3):
        wait_half(i)
    for i in range(3):
        quarter_s[i] = (acc[i, rows_of(part_chip)] + half_r[i, 1 - z_low].astype(F32)).astype(BF16)
        quarter(i).start()
    sum_z[3] = per_token_z(3).astype(BF16)
    remote(sum_z.at[3], got_z.at[3], sum_send.at[1], got_z_sem.at[3], z_from).start()
    step_sum_y(1, 0, y_prev)
    step_sum_y(7, 4, y_next)
    sum_z[1] = per_token_z(1).astype(BF16)
    remote(sum_z.at[1], got_z.at[1], sum_send.at[1], got_z_sem.at[1], z_from).start()
    own_z2 = per_token_z(2)
    pltpu.make_async_copy(got_z.at[3], got_z.at[3], got_z_sem.at[3]).wait()
    sum_z[2] = (own_z2 + got_z[3].astype(F32)).astype(BF16)
    remote(sum_z.at[2], got_z.at[2], sum_send.at[1], got_z_sem.at[2], z_back).start()
    own_y = per_token_y(0)
    own_z = per_token_z(0)
    wait_got_y(0)
    wait_got_y(4)
    d_tok[:, 0:D // 2] = (own_y + got_y[0].astype(F32) + got_y[4].astype(F32)).astype(BF16)
    for i in range(3):
        quarter(i).wait()
    outs = (g_gate, g_up, g_down)
    for i in range(3):
        outs[i][...] = acc[i, rows_of(part)] + half_r[i, z_low].astype(F32) + quarter_r[i].astype(F32)
    pltpu.make_async_copy(got_z.at[1], got_z.at[1], got_z_sem.at[1]).wait()
    pltpu.make_async_copy(got_z.at[2], got_z.at[2], got_z_sem.at[2]).wait()
    d_tok[:, D // 2:D] = (own_z + got_z[1].astype(F32) + got_z[2].astype(F32)).astype(BF16)

    def wait_sent(ref, sem):
        pltpu.make_async_copy(ref, ref, sem).wait()

    wait_sent(send_t.at[pl.ds(0, ROWS - 64)], send_sem.at[0])
    wait_sent(send_g.at[pl.ds(0, ROWS - 32)], send_sem.at[1])
    wait_sent(part_y.at[pl.ds(0, ROWS - 64)], ret_send.at[0])
    wait_sent(part_z.at[pl.ds(0, ROWS - 32)], ret_send.at[1])
    wait_sent(ring_t.at[pl.ds(1, 7)], ring_send)
    wait_sent(gath_g.at[pl.ds(1, 3)], gath_send)
    wait_sent(metas, id_send.at[0])
    wait_sent(all_ids, id_send.at[1])
    wait_sent(sum_y.at[pl.ds(1, 7)], sum_send.at[0])
    wait_sent(sum_z.at[pl.ds(1, 3)], sum_send.at[1])
    for _ in range(3):
        wait_sent(w_chip, w_send)


def per_device(tokens, out_grad, expert_ids, gate_scores, w_gate, w_up, w_down):
    vmem = pl.BlockSpec(memory_space=pltpu.VMEM)
    block = jax.ShapeDtypeStruct((DQ, HID), F32)
    dma = pltpu.SemaphoreType.DMA
    half = D // 2
    d_tokens, gate, up, down = pl.pallas_call(
        body,
        out_shape=(jax.ShapeDtypeStruct((TOK, D), BF16), block, block, block),
        in_specs=[pl.BlockSpec(memory_space=pl.ANY)] * 7,
        out_specs=(vmem,) * 4,
        scratch_shapes=[
            pltpu.VMEM((TOK, D), BF16),
            pltpu.VMEM((TOK, D), BF16),
            pltpu.VMEM((16, TOK), jnp.int32),
            pltpu.VMEM((ROWS, EXPERTS), BF16),
            pltpu.VMEM((ROWS, TOK), BF16),
            pltpu.VMEM((ROWS, TOK), BF16),
            pltpu.VMEM((ROWS, TOK), BF16),
            pltpu.VMEM((8, TOK, D), BF16),
            pltpu.VMEM((8, 8, TOK), jnp.int32),
            pltpu.VMEM((4, TOK, D), BF16),
            pltpu.VMEM((4, 16, TOK), jnp.int32),
            pltpu.VMEM((ROWS, D), BF16),
            pltpu.VMEM((ROWS, D), BF16),
            pltpu.VMEM((ROWS, D), BF16),
            pltpu.VMEM((ROWS, D), BF16),
            pltpu.VMEM((ROWS, half), BF16),
            pltpu.VMEM((ROWS, half), BF16),
            pltpu.VMEM((8, TOK, half), BF16),
            pltpu.VMEM((4, 256, half), BF16),
            pltpu.VMEM((8, TOK, half), BF16),
            pltpu.VMEM((4, TOK, half), BF16),
            pltpu.VMEM((8, TOK, half), BF16),
            pltpu.VMEM((4, TOK, half), BF16),
            pltpu.VMEM((3, D, HID), BF16),
            pltpu.VMEM((3, D, HID), F32),
            pltpu.VMEM((3, 2, DQ, HID), BF16),
            pltpu.VMEM((3, 2, DQ, HID), BF16),
            pltpu.VMEM((3, DQ, HID), BF16),
            pltpu.VMEM((3, DQ, HID), BF16),
            dma((7,)),
            dma,
            dma((8, SUB)),
            dma,
            dma((4,)),
            dma((2,)),
            dma((2,)),
            dma((2,)),
            dma((CHUNKS,)),
            dma((CHUNKS,)),
            dma,
            dma((3,)),
            dma((2,)),
            dma((8,)),
            dma((4,)),
            dma((2,)),
            dma((8,)),
            dma((4,)),
            dma((6,)),
            dma((6,)),
        ],
        compiler_params=pltpu.CompilerParams(
            collective_id=0, has_side_effects=True, vmem_limit_bytes=40 << 20),
        name="expert_layer_backward",
    )(tokens, out_grad, expert_ids.T, gate_scores.T, w_gate[0], w_up[0], w_down[0])
    return d_tokens, gate[None], up[None], down[None]


def solution(mesh):
    rows = P(("expert", "dp"), None)
    blocks = P(("expert", "dp"), None, None)
    return jax.shard_map(
        per_device,
        mesh=mesh,
        in_specs=(rows, rows, rows, rows, blocks, blocks, blocks),
        out_specs=(rows, blocks, blocks, blocks),
        check_vma=False,
    )
```

```python
import jax
import jax.numpy as jnp
from jax import lax
from jax.experimental import pallas as pl
from jax.experimental.pallas import tpu as pltpu
from jax.sharding import PartitionSpec as P

MESH = pl.DeviceIdType.MESH
TOK = 128
D = 1024
HID = 384
EXPERTS = 128
ROWS = 1024
CHUNKS = 4
SUB = 2
CUT = 768
CHUNK = ROWS // CHUNKS
DQ = 256
F32 = jnp.float32
BF16 = jnp.bfloat16


def dot(lhs, rhs, contract):
    return lax.dot_general(lhs, rhs, (contract, ((), ())), preferred_element_type=F32)


def remote(src, dst, send_sem, recv_sem, device):
    return pltpu.make_async_remote_copy(
        src_ref=src, dst_ref=dst, send_sem=send_sem, recv_sem=recv_sem,
        device_id=device, device_id_type=MESH)


def device_at(x, y, z_pair, z_low, core):
    return {"expert": y * 4 + z_pair, "dp": x * 4 + z_low * 2 + core}


def dy_of(chunk, side):
    return jnp.where(side == 0, 4 - chunk, jnp.where(chunk == 0, 0, 4 + chunk))


def place_of(dy):
    return {4: (0, 0), 0: (0, 1), 3: (1, 0), 5: (1, 1), 2: (2, 0), 6: (2, 1), 1: (3, 0), 7: (3, 1)}[dy]


def slot_of(chunk, side, dx, j):
    return chunk * 32 + side * 16 + dx * 4 + j


def one_hot(condition):
    return jnp.where(condition, 1.0, 0.0)


def routing(id_blocks, expert_at, score_blocks, spread):
    each = EXPERTS // len(id_blocks)
    local = lax.broadcasted_iota(jnp.int32, (each, TOK), 0)
    experts = expert_at(local)
    members, gates = [], []
    for n, ids in enumerate(id_blocks):
        if score_blocks is not None:
            score = score_blocks[n].astype(F32)
            gate = (score / jnp.sum(score, axis=0, keepdims=True)).astype(BF16).astype(F32)
        member = jnp.zeros((each, TOK), F32)
        gate_of = jnp.zeros((each, TOK), F32)
        for k in range(8):
            hit = one_hot(experts == ids[k:k + 1, :])
            member = member + hit
            if score_blocks is not None:
                gate_of = gate_of + hit * gate[k:k + 1, :]
        members.append(member)
        gates.append(gate_of)
    member = jnp.concatenate(members, axis=0).astype(BF16)
    before = one_hot(lax.broadcasted_iota(jnp.int32, (TOK, TOK), 0)
                     < lax.broadcasted_iota(jnp.int32, (TOK, TOK), 1)).astype(BF16)
    rank = dot(member, before, ((1,), (0,)))
    wide_member = dot(spread, member, ((1,), (0,)))
    wide_rank = dot(spread, rank.astype(BF16), ((1,), (0,)))
    slot_rank = lax.rem(lax.broadcasted_iota(jnp.int32, (ROWS, TOK), 0), 8).astype(F32)
    chosen = jnp.where(wide_rank == slot_rank, wide_member, 0.0)
    if score_blocks is None:
        return chosen.astype(BF16), None
    wide_gate = dot(spread, jnp.concatenate(gates, axis=0).astype(BF16), ((1,), (0,)))
    return chosen.astype(BF16), (chosen * wide_gate).astype(BF16)


def body(tok_in, grad_in, ids_in, scores_in, wg, wu, wd, d_tok, g_gate, g_up, g_down,
         tok, grad, meta, spread, pick_y, pick_z, gated_z, ring_t, ring_i, gath_g, gath_m,
         send_t, send_g, recv_t, recv_g, part_y, part_z, ret_y, ret_z, sum_y, sum_z, got_y, got_z, weights, acc,
         half_s, half_r, quarter_s, quarter_r,
         load_sem, ring_send, ring_recv, gath_send, gath_recv, id_send, id_recv,
         send_sem, recv_t_sem, recv_g_sem, w_send, w_recv, ret_send, ret_y_sem, ret_z_sem,
         sum_send, got_y_sem, got_z_sem, red_send, red_recv):
    e_pos = lax.axis_index("expert")
    d_pos = lax.axis_index("dp")
    y, z_pair = e_pos // 4, lax.rem(e_pos, 4)
    x, part = d_pos // 4, lax.rem(d_pos, 4)
    z_low, core = part // 2, lax.rem(part, 2)
    other_core = device_at(x, y, z_pair, z_low, 1 - core)
    other_chip = device_at(x, y, z_pair, 1 - z_low, core)
    part_core = z_low * 2 + 1 - core
    part_chip = (1 - z_low) * 2 + core
    part_far = (1 - z_low) * 2 + 1 - core
    dz_near = jnp.where(z_low == 0, 1, 3)
    dz_back = 4 - dz_near
    y_next = device_at(x, lax.rem(y + 1, 8), z_pair, z_low, core)
    y_prev = device_at(x, lax.rem(y + 7, 8), z_pair, z_low, core)
    z_near = device_at(x, y, lax.rem(z_pair + dz_near, 4), z_low, core)
    z_back = device_at(x, y, lax.rem(z_pair + dz_back, 4), 1 - z_low, core)
    z_far = device_at(x, y, lax.rem(z_pair + 2, 4), 1 - z_low, core)

    def rows_of(p):
        return pl.ds(pl.multiple_of(p * DQ, DQ), DQ)

    z_from = device_at(x, y, lax.rem(z_pair + dz_back, 4), z_low, core)

    entry = pltpu.get_barrier_semaphore()

    def greet(target):
        pl.semaphore_signal(entry, inc=1, device_id=target, device_id_type=MESH)

    def greet_xy(index, carry):
        greet(device_at(lax.rem(x + lax.rem(index, 4), 4), lax.rem(y + index // 4, 8), z_pair, z_low, core))
        return carry

    def greet_xz(index, carry):
        x_to = lax.rem(x + index, 4)
        greet(device_at(x_to, y, lax.rem(z_pair + dz_near, 4), z_low, core))
        greet(device_at(x_to, y, lax.rem(z_pair + dz_back, 4), z_low, core))
        greet(device_at(x_to, y, lax.rem(z_pair + dz_back, 4), 1 - z_low, core))
        greet(device_at(x_to, y, lax.rem(z_pair + 2, 4), 1 - z_low, core))
        return carry

    greet(other_core)
    greet(other_chip)
    lax.fori_loop(0, 4, greet_xz, 0)
    lax.fori_loop(1, 32, greet_xy, 0)

    own_weights = weights.at[:, rows_of(part)]
    loads = [pltpu.make_async_copy(grad_in, grad, load_sem.at[0]),
             pltpu.make_async_copy(tok_in, tok, load_sem.at[1]),
             pltpu.make_async_copy(ids_in, meta.at[pl.ds(0, 8)], load_sem.at[2]),
             pltpu.make_async_copy(scores_in, meta.at[pl.ds(8, 8)], load_sem.at[3])]
    for i, ref in enumerate((wg, wu, wd)):
        loads.append(pltpu.make_async_copy(ref, weights.at[i, rows_of(part)], load_sem.at[4 + i]))
    for load in loads:
        load.start()
    spread[...] = one_hot(lax.broadcasted_iota(jnp.int32, (ROWS, EXPERTS), 0) // 8
                          == lax.broadcasted_iota(jnp.int32, (ROWS, EXPERTS), 1)).astype(BF16)
    acc[...] = jnp.zeros_like(acc)
    for load in loads:
        load.wait()
    pl.semaphore_wait(entry, 49)

    remote(grad, gath_g.at[2], gath_send, gath_recv.at[2], z_back).start()
    remote(grad, gath_g.at[1], gath_send, gath_recv.at[1], z_near).start()
    for n in range(SUB):
        rows = pl.ds(n * (TOK // SUB), TOK // SUB)
        remote(tok.at[rows], ring_t.at[1, rows], ring_send, ring_recv.at[1, n], y_next).start()
        remote(tok.at[rows], ring_t.at[7, rows], ring_send, ring_recv.at[7, n], y_prev).start()
    for j, target in ((2, z_back), (1, z_near), (3, z_far)):
        remote(meta, gath_m.at[j], id_send.at[0], id_recv.at[0], target).start()

    def send_ids(dy, carry):
        target = device_at(x, lax.rem(y + dy, 8), z_pair, z_low, core)
        remote(meta.at[pl.ds(0, 8)], ring_i.at[dy], id_send.at[1], id_recv.at[1], target).start()
        return carry

    lax.fori_loop(1, 8, send_ids, 0)
    remote(own_weights, own_weights, w_send, w_recv.at[0], other_chip).start()
    remote(own_weights, own_weights, w_send, w_recv.at[1], other_core).start()

    def send_tokens(dy):
        block = tok if dy == 0 else ring_t.at[dy]
        chunk, side = place_of(dy)
        rows = pl.ds(dy * TOK, TOK)
        send_t[rows] = dot(pick_y[rows], block[...], ((1,), (0,))).astype(BF16)

        def one(index, carry):
            j, dx = lax.rem(index, 4), index // 4
            dz = jnp.where(j == 0, 0, jnp.where(j == 3, 2, jnp.where(j == 1, dz_near, dz_back)))
            z_low_to = jnp.where(j < 2, z_low, 1 - z_low)
            x_to, z_to = lax.rem(x + dx, 4), lax.rem(z_pair + dz, 4)
            src = pl.ds(pl.multiple_of(dy * TOK + (z_to * 4 + x_to) * 8, 8), 8)
            dst = pl.ds(pl.multiple_of(slot_of(chunk, side, dx, j) * 8, 8), 8)

            @pl.when(index == 0)
            def _():
                pltpu.make_async_copy(send_t.at[src], recv_t.at[dst], recv_t_sem.at[chunk]).start()

            @pl.when(index > 0)
            def _():
                target = device_at(x_to, y, z_to, z_low_to, core)
                remote(send_t.at[src], recv_t.at[dst], send_sem.at[0], recv_t_sem.at[chunk], target).start()

            return carry

        lax.fori_loop(0, 16, one, 0)

    def scale_grads(j):
        block = grad if j == 0 else gath_g.at[j]
        rows = pl.ds(j * 256, 256)
        send_g[rows] = dot(gated_z[rows], block[...], ((1,), (0,))).astype(BF16)

    def send_grads(chunk):
        def one(index, carry):
            side, j, dx = lax.rem(index, 2), lax.rem(index // 2, 4), index // 8
            dy = dy_of(chunk, side)
            x_to, y_to = lax.rem(x + dx, 4), lax.rem(y + dy, 8)
            src = pl.ds(pl.multiple_of(j * 256 + (y_to * 4 + x_to) * 8, 8), 8)
            dst = pl.ds(pl.multiple_of(slot_of(chunk, side, dx, j) * 8, 8), 8)
            here = (dx + dy) == 0

            @pl.when(here)
            def _():
                pltpu.make_async_copy(send_g.at[src], recv_g.at[dst], recv_g_sem.at[chunk]).start()

            @pl.when(jnp.logical_not(here))
            def _():
                target = device_at(x_to, y_to, z_pair, z_low, core)
                remote(send_g.at[src], recv_g.at[dst], send_sem.at[1], recv_g_sem.at[chunk], target).start()

            return carry

        lax.fori_loop(0, 32, one, 0)

    def ring_rows(n):
        return pl.ds(n * (TOK // SUB), TOK // SUB)

    def wait_ring(dy, n):
        ref = ring_t.at[dy, ring_rows(n)]
        pltpu.make_async_copy(ref, ref, ring_recv.at[dy, n]).wait()

    def pass_on(dy, to, n, target):
        remote(ring_t.at[dy, ring_rows(n)], ring_t.at[to, ring_rows(n)],
               ring_send, ring_recv.at[to, n], target).start()

    def wait_gath(j):
        pltpu.make_async_copy(gath_g.at[j], gath_g.at[j], gath_recv.at[j]).wait()

    metas = gath_m.at[pl.ds(1, 3)]
    pltpu.make_async_copy(metas, metas, id_recv.at[0]).wait()
    all_ids = ring_i.at[pl.ds(1, 7)]
    pltpu.make_async_copy(all_ids, all_ids, id_recv.at[1]).wait()
    pick_z[...], gated_z[...] = routing([meta[0:8]] + [gath_m[j, 0:8] for j in range(1, 4)],
                                        lambda e: (e // 4) * 16 + z_pair * 4 + lax.rem(e, 4),
                                        [meta[8:16]] + [gath_m[j, 8:16] for j in range(1, 4)], spread[...])
    def make_pick_y():
        pick_y[...], _ = routing([meta[0:8]] + [ring_i[dy] for dy in range(1, 8)], lambda e: y * 16 + e, None, spread[...])

    def hops(step):
        for n in range(SUB):
            wait_ring(step, n)
            if step < 3 or n < SUB // 2:
                pass_on(step, step + 1, n, y_next)
            wait_ring(8 - step, n)
            if step < 3 or n >= SUB // 2:
                pass_on(8 - step, 7 - step, n, y_prev)

    def relay():
        wait_gath(2)
        remote(gath_g.at[2], gath_g.at[3], gath_send, gath_recv.at[3], z_near).start()

    w_chip = weights.at[:, rows_of(part_chip)]

    def pass_weights():
        pltpu.make_async_copy(w_chip, w_chip, w_recv.at[0]).wait()
        remote(w_chip, w_chip, w_send, w_recv.at[2], other_core).start()

    def last_block():
        for n in range(SUB):
            wait_ring(4, n)

    def wait_weights():
        for n, p in ((1, part_core), (2, part_far)):
            ref = weights.at[:, rows_of(p)]
            pltpu.make_async_copy(ref, ref, w_recv.at[n]).wait()

    def compute(c):
        rows = pl.ds(c * CHUNK, CHUNK)
        pltpu.make_async_copy(recv_t.at[rows], recv_t.at[rows], recv_t_sem.at[c]).wait()
        pltpu.make_async_copy(recv_g.at[rows], recv_g.at[rows], recv_g_sem.at[c]).wait()
        row_in = recv_t[rows]
        scaled = recv_g[rows]
        a = dot(row_in, weights[0], ((1,), (0,)))
        b = dot(row_in, weights[1], ((1,), (0,)))
        back = dot(scaled, weights[2], ((1,), (0,)))
        sig = jax.nn.sigmoid(a)
        silu = a * sig
        hidden = (silu * b).astype(BF16)
        gate_back = (back * b * sig * (1.0 + a * (1.0 - sig))).astype(BF16)
        up_back = (back * silu).astype(BF16)
        token_part = (dot(gate_back, weights[0], ((1,), (1,)))
                      + dot(up_back, weights[1], ((1,), (1,)))).astype(BF16)
        part_y[rows] = token_part[:, :CUT]
        part_z[rows] = token_part[:, CUT:]

        def give_back(index, carry):
            side, j, dx = lax.rem(index, 2), lax.rem(index // 2, 4), index // 8
            dy = dy_of(c, side)
            dz = jnp.where(j == 0, 0, jnp.where(j == 3, 2, dz_near))
            z_low_from = jnp.where(j < 2, z_low, 1 - z_low)
            x_to, y_to, z_to = lax.rem(x + 4 - dx, 4), lax.rem(y + 8 - dy, 8), lax.rem(z_pair + 4 - dz, 4)
            src = pl.ds(pl.multiple_of(slot_of(c, side, dx, j) * 8, 8), 8)
            dst_y = ret_y.at[dy, pl.ds(pl.multiple_of((z_pair * 4 + x) * 8, 8), 8)]
            dst_z = ret_z.at[j, pl.ds(pl.multiple_of((y * 4 + x) * 8, 8), 8)]
            stays_y = (dx + j) == 0
            stays_z = (dx + dy) == 0

            @pl.when(stays_z)
            def _():
                pltpu.make_async_copy(part_z.at[src], dst_z, ret_z_sem.at[j]).start()

            @pl.when(jnp.logical_not(stays_z))
            def _():
                target = device_at(x_to, y_to, z_pair, z_low, core)
                remote(part_z.at[src], dst_z, ret_send.at[1], ret_z_sem.at[j], target).start()

            @pl.when(stays_y)
            def _():
                pltpu.make_async_copy(part_y.at[src], dst_y, ret_y_sem.at[dy]).start()

            @pl.when(jnp.logical_not(stays_y))
            def _():
                target = device_at(x_to, y, z_to, z_low_from, core)
                remote(part_y.at[src], dst_y, ret_send.at[0], ret_y_sem.at[dy], target).start()

            return carry

        lax.fori_loop(0, 32, give_back, 0)
        acc[0] += dot(row_in, gate_back, ((0,), (0,)))
        acc[1] += dot(row_in, up_back, ((0,), (0,)))
        if c == CHUNKS - 1:
            start_half(0)
            start_half(1)
        acc[2] += dot(scaled, hidden, ((0,), (0,)))
        if c == CHUNKS - 1:
            start_half(2)

    def per_token_y(dy):
        pltpu.make_async_copy(ret_y.at[dy], ret_y.at[dy], ret_y_sem.at[dy]).wait()
        return dot(pick_y[pl.ds(dy * TOK, TOK)], ret_y[dy], ((0,), (0,)))

    def per_token_z(j):
        pltpu.make_async_copy(ret_z.at[j], ret_z.at[j], ret_z_sem.at[j]).wait()
        return dot(pick_z[pl.ds(j * 256, 256)], ret_z[j], ((0,), (0,)))

    low, high = pl.ds(0, TOK // 2), pl.ds(TOK // 2, TOK // 2)

    def wait_got_y(slot, rows=None):
        ref = got_y.at[slot] if rows is None else got_y.at[slot, rows]
        pltpu.make_async_copy(ref, ref, got_y_sem.at[slot]).wait()

    def start_sum_y():
        sum_y[4] = per_token_y(4).astype(BF16)
        remote(sum_y.at[4, low], got_y.at[3, low], sum_send.at[0], got_y_sem.at[3], y_prev).start()
        remote(sum_y.at[4, high], got_y.at[5, high], sum_send.at[0], got_y_sem.at[5], y_next).start()

    def step_sum_y(dy, to, target):
        total = per_token_y(dy)
        if dy == 3:
            wait_got_y(3, low)
            half = TOK // 2
            sum_y[3, 0:half] = (total[0:half] + got_y[3, 0:half].astype(F32)).astype(BF16)
            sum_y[3, half:TOK] = total[half:TOK].astype(BF16)
        elif dy == 5:
            wait_got_y(5, high)
            half = TOK // 2
            sum_y[5, 0:half] = total[0:half].astype(BF16)
            sum_y[5, half:TOK] = (total[half:TOK] + got_y[5, half:TOK].astype(F32)).astype(BF16)
        else:
            wait_got_y(dy)
            sum_y[dy] = (total + got_y[dy].astype(F32)).astype(BF16)
        remote(sum_y.at[dy], got_y.at[to], sum_send.at[0], got_y_sem.at[to], target).start()

    def half(i):
        return remote(half_s.at[i], half_r.at[i], red_send.at[i], red_recv.at[i], other_core)

    def quarter(i):
        return remote(quarter_s.at[i], quarter_r.at[i], red_send.at[3 + i], red_recv.at[3 + i], other_chip)

    def start_half(i):
        for zl in range(2):
            half_s[i, zl] = acc[i, rows_of(zl * 2 + 1 - core)].astype(BF16)
        half(i).start()

    def wait_half(i):
        half(i).wait()

    hops(1)
    relay()
    make_pick_y()
    send_tokens(0)
    scale_grads(0)
    hops(2)
    scale_grads(2)
    send_tokens(1)
    send_tokens(7)
    pass_weights()
    wait_gath(1)
    scale_grads(1)
    hops(3)
    wait_gath(3)
    scale_grads(3)
    send_grads(0)
    send_tokens(3)
    send_tokens(5)
    last_block()
    send_tokens(4)
    send_grads(1)
    send_tokens(2)
    send_tokens(6)
    send_grads(2)
    wait_weights()
    compute(0)
    send_grads(3)
    compute(1)
    start_sum_y()
    compute(2)
    step_sum_y(3, 2, y_prev)
    step_sum_y(5, 6, y_next)
    compute(3)
    for i in range(3):
        wait_half(i)
        quarter_s[i] = (acc[i, rows_of(part_chip)] + half_r[i, 1 - z_low].astype(F32)).astype(BF16)
        quarter(i).start()
    step_sum_y(2, 1, y_prev)
    step_sum_y(6, 7, y_next)
    sum_z[3] = per_token_z(3).astype(BF16)
    remote(sum_z.at[3], got_z.at[3], sum_send.at[1], got_z_sem.at[3], z_from).start()
    step_sum_y(1, 0, y_prev)
    step_sum_y(7, 4, y_next)
    sum_z[1] = per_token_z(1).astype(BF16)
    remote(sum_z.at[1], got_z.at[1], sum_send.at[1], got_z_sem.at[1], z_from).start()
    own_z2 = per_token_z(2)
    pltpu.make_async_copy(got_z.at[3], got_z.at[3], got_z_sem.at[3]).wait()
    sum_z[2] = (own_z2 + got_z[3].astype(F32)).astype(BF16)
    remote(sum_z.at[2], got_z.at[2], sum_send.at[1], got_z_sem.at[2], z_back).start()
    own_y = per_token_y(0)
    own_z = per_token_z(0)
    wait_got_y(0)
    wait_got_y(4)
    d_tok[:, 0:CUT] = (own_y + got_y[0].astype(F32) + got_y[4].astype(F32)).astype(BF16)
    for i in range(3):
        quarter(i).wait()
    outs = (g_gate, g_up, g_down)
    for i in range(3):
        outs[i][...] = acc[i, rows_of(part)] + half_r[i, z_low].astype(F32) + quarter_r[i].astype(F32)
    pltpu.make_async_copy(got_z.at[1], got_z.at[1], got_z_sem.at[1]).wait()
    pltpu.make_async_copy(got_z.at[2], got_z.at[2], got_z_sem.at[2]).wait()
    d_tok[:, CUT:D] = (own_z + got_z[1].astype(F32) + got_z[2].astype(F32)).astype(BF16)

    def wait_sent(ref, sem):
        pltpu.make_async_copy(ref, ref, sem).wait()

    wait_sent(send_t.at[pl.ds(0, ROWS - 64)], send_sem.at[0])
    wait_sent(send_g.at[pl.ds(0, ROWS - 32)], send_sem.at[1])
    wait_sent(part_y.at[pl.ds(0, ROWS - 64)], ret_send.at[0])
    wait_sent(part_z.at[pl.ds(0, ROWS - 32)], ret_send.at[1])
    wait_sent(ring_t.at[pl.ds(1, 7)], ring_send)
    wait_sent(gath_g.at[pl.ds(1, 3)], gath_send)
    wait_sent(metas, id_send.at[0])
    wait_sent(all_ids, id_send.at[1])
    wait_sent(sum_y.at[pl.ds(1, 7)], sum_send.at[0])
    wait_sent(sum_z.at[pl.ds(1, 3)], sum_send.at[1])
    for _ in range(3):
        wait_sent(w_chip, w_send)


def per_device(tokens, out_grad, expert_ids, gate_scores, w_gate, w_up, w_down):
    vmem = pl.BlockSpec(memory_space=pltpu.VMEM)
    block = jax.ShapeDtypeStruct((DQ, HID), F32)
    dma = pltpu.SemaphoreType.DMA
    operands = [pltpu.with_memory_space_constraint(value, pltpu.HBM) for value in (
        tokens, out_grad, expert_ids.T, gate_scores.T, w_gate[0], w_up[0], w_down[0])]
    d_tokens, gate, up, down = pl.pallas_call(
        body,
        out_shape=(jax.ShapeDtypeStruct((TOK, D), BF16), block, block, block),
        in_specs=[pl.BlockSpec(memory_space=pl.ANY)] * 7,
        out_specs=(vmem,) * 4,
        scratch_shapes=[
            pltpu.VMEM((TOK, D), BF16),
            pltpu.VMEM((TOK, D), BF16),
            pltpu.VMEM((16, TOK), jnp.int32),
            pltpu.VMEM((ROWS, EXPERTS), BF16),
            pltpu.VMEM((ROWS, TOK), BF16),
            pltpu.VMEM((ROWS, TOK), BF16),
            pltpu.VMEM((ROWS, TOK), BF16),
            pltpu.VMEM((8, TOK, D), BF16),
            pltpu.VMEM((8, 8, TOK), jnp.int32),
            pltpu.VMEM((4, TOK, D), BF16),
            pltpu.VMEM((4, 16, TOK), jnp.int32),
            pltpu.VMEM((ROWS, D), BF16),
            pltpu.VMEM((ROWS, D), BF16),
            pltpu.VMEM((ROWS, D), BF16),
            pltpu.VMEM((ROWS, D), BF16),
            pltpu.VMEM((ROWS, CUT), BF16),
            pltpu.VMEM((ROWS, D - CUT), BF16),
            pltpu.VMEM((8, TOK, CUT), BF16),
            pltpu.VMEM((4, 256, D - CUT), BF16),
            pltpu.VMEM((8, TOK, CUT), BF16),
            pltpu.VMEM((4, TOK, D - CUT), BF16),
            pltpu.VMEM((8, TOK, CUT), BF16),
            pltpu.VMEM((4, TOK, D - CUT), BF16),
            pltpu.VMEM((3, D, HID), BF16),
            pltpu.VMEM((3, D, HID), F32),
            pltpu.VMEM((3, 2, DQ, HID), BF16),
            pltpu.VMEM((3, 2, DQ, HID), BF16),
            pltpu.VMEM((3, DQ, HID), BF16),
            pltpu.VMEM((3, DQ, HID), BF16),
            dma((7,)),
            dma,
            dma((8, SUB)),
            dma,
            dma((4,)),
            dma((2,)),
            dma((2,)),
            dma((2,)),
            dma((CHUNKS,)),
            dma((CHUNKS,)),
            dma,
            dma((3,)),
            dma((2,)),
            dma((8,)),
            dma((4,)),
            dma((2,)),
            dma((8,)),
            dma((4,)),
            dma((6,)),
            dma((6,)),
        ],
        compiler_params=pltpu.CompilerParams(
            collective_id=0, has_side_effects=True, vmem_limit_bytes=40 << 20),
        name="expert_layer_backward",
    )(*operands)
    return d_tokens, gate[None], up[None], down[None]


def solution(mesh):
    rows = P(("expert", "dp"), None)
    blocks = P(("expert", "dp"), None, None)
    return jax.shard_map(
        per_device,
        mesh=mesh,
        in_specs=(rows, rows, rows, rows, blocks, blocks, blocks),
        out_specs=(rows, blocks, blocks, blocks),
        check_vma=False,
    )
```

```python
import jax
import jax.numpy as jnp
from jax import lax
from jax.experimental import pallas as pl
from jax.experimental.pallas import tpu as pltpu
from jax.sharding import PartitionSpec as P

MESH = pl.DeviceIdType.MESH
TOK = 128
D = 1024
HID = 384
EXPERTS = 128
ROWS = 1024
CHUNKS = 4
SUB = 2
CUT = 768
CHUNK = ROWS // CHUNKS
DQ = 256
F32 = jnp.float32
BF16 = jnp.bfloat16


def dot(lhs, rhs, contract):
    return lax.dot_general(lhs, rhs, (contract, ((), ())), preferred_element_type=F32)


def remote(src, dst, send_sem, recv_sem, device):
    return pltpu.make_async_remote_copy(
        src_ref=src, dst_ref=dst, send_sem=send_sem, recv_sem=recv_sem,
        device_id=device, device_id_type=MESH)


def device_at(x, y, z_pair, z_low, core):
    return {"expert": y * 4 + z_pair, "dp": x * 4 + z_low * 2 + core}


def dy_of(chunk, side):
    return jnp.where(side == 0, 4 - chunk, jnp.where(chunk == 0, 0, 4 + chunk))


def place_of(dy):
    return {4: (0, 0), 0: (0, 1), 3: (1, 0), 5: (1, 1), 2: (2, 0), 6: (2, 1), 1: (3, 0), 7: (3, 1)}[dy]


def slot_of(chunk, side, dx, j):
    return chunk * 32 + side * 16 + dx * 4 + j


def one_hot(condition):
    return jnp.where(condition, 1.0, 0.0)


def routing(id_blocks, expert_at, score_blocks, spread):
    each = EXPERTS // len(id_blocks)
    local = lax.broadcasted_iota(jnp.int32, (each, TOK), 0)
    experts = expert_at(local)
    members, gates = [], []
    for n, ids in enumerate(id_blocks):
        if score_blocks is not None:
            score = score_blocks[n].astype(F32)
            gate = (score / jnp.sum(score, axis=0, keepdims=True)).astype(BF16).astype(F32)
        member = jnp.zeros((each, TOK), F32)
        gate_of = jnp.zeros((each, TOK), F32)
        for k in range(8):
            hit = one_hot(experts == ids[k:k + 1, :])
            member = member + hit
            if score_blocks is not None:
                gate_of = gate_of + hit * gate[k:k + 1, :]
        members.append(member)
        gates.append(gate_of)
    member = jnp.concatenate(members, axis=0).astype(BF16)
    before = one_hot(lax.broadcasted_iota(jnp.int32, (TOK, TOK), 0)
                     < lax.broadcasted_iota(jnp.int32, (TOK, TOK), 1)).astype(BF16)
    rank = dot(member, before, ((1,), (0,)))
    wide_member = dot(spread, member, ((1,), (0,)))
    wide_rank = dot(spread, rank.astype(BF16), ((1,), (0,)))
    slot_rank = lax.rem(lax.broadcasted_iota(jnp.int32, (ROWS, TOK), 0), 8).astype(F32)
    chosen = jnp.where(wide_rank == slot_rank, wide_member, 0.0)
    if score_blocks is None:
        return chosen.astype(BF16), None
    wide_gate = dot(spread, jnp.concatenate(gates, axis=0).astype(BF16), ((1,), (0,)))
    return chosen.astype(BF16), (chosen * wide_gate).astype(BF16)


def body(tok_in, grad_in, ids_in, scores_in, wg, wu, wd, d_tok, g_gate, g_up, g_down,
         tok, grad, meta, spread, pick_y, pick_z, gated_z, ring_t, ring_i, gath_g, gath_m,
         send_t, send_g, recv_t, recv_g, part_y, part_z, ret_y, ret_z, sum_y, sum_z, got_y, got_z, weights, acc,
         half_s, half_r, quarter_s, quarter_r,
         load_sem, ring_send, ring_recv, gath_send, gath_recv, id_send, id_recv,
         send_sem, recv_t_sem, recv_g_sem, w_send, w_recv, ret_send, ret_y_sem, ret_z_sem,
         sum_send, got_y_sem, got_z_sem, red_send, red_recv):
    e_pos = lax.axis_index("expert")
    d_pos = lax.axis_index("dp")
    y, z_pair = e_pos // 4, lax.rem(e_pos, 4)
    x, part = d_pos // 4, lax.rem(d_pos, 4)
    z_low, core = part // 2, lax.rem(part, 2)
    other_core = device_at(x, y, z_pair, z_low, 1 - core)
    other_chip = device_at(x, y, z_pair, 1 - z_low, core)
    part_core = z_low * 2 + 1 - core
    part_chip = (1 - z_low) * 2 + core
    part_far = (1 - z_low) * 2 + 1 - core
    dz_near = jnp.where(z_low == 0, 1, 3)
    dz_back = 4 - dz_near
    y_next = device_at(x, lax.rem(y + 1, 8), z_pair, z_low, core)
    y_prev = device_at(x, lax.rem(y + 7, 8), z_pair, z_low, core)
    z_near = device_at(x, y, lax.rem(z_pair + dz_near, 4), z_low, core)
    z_back = device_at(x, y, lax.rem(z_pair + dz_back, 4), 1 - z_low, core)
    z_far = device_at(x, y, lax.rem(z_pair + 2, 4), 1 - z_low, core)

    def rows_of(p):
        return pl.ds(pl.multiple_of(p * DQ, DQ), DQ)

    z_from = device_at(x, y, lax.rem(z_pair + dz_back, 4), z_low, core)

    entry = pltpu.get_barrier_semaphore()

    def greet(target):
        pl.semaphore_signal(entry, inc=1, device_id=target, device_id_type=MESH)

    def greet_xy(index, carry):
        greet(device_at(lax.rem(x + lax.rem(index, 4), 4), lax.rem(y + index // 4, 8), z_pair, z_low, core))
        return carry

    def greet_xz(index, carry):
        x_to = lax.rem(x + index, 4)
        greet(device_at(x_to, y, lax.rem(z_pair + dz_near, 4), z_low, core))
        greet(device_at(x_to, y, lax.rem(z_pair + dz_back, 4), z_low, core))
        greet(device_at(x_to, y, lax.rem(z_pair + dz_back, 4), 1 - z_low, core))
        greet(device_at(x_to, y, lax.rem(z_pair + 2, 4), 1 - z_low, core))
        return carry

    greet(other_core)
    greet(other_chip)
    lax.fori_loop(0, 4, greet_xz, 0)
    lax.fori_loop(1, 32, greet_xy, 0)

    own_weights = weights.at[:, rows_of(part)]
    loads = [pltpu.make_async_copy(grad_in, grad, load_sem.at[0]),
             pltpu.make_async_copy(tok_in, tok, load_sem.at[1]),
             pltpu.make_async_copy(ids_in, meta.at[pl.ds(0, 8)], load_sem.at[2]),
             pltpu.make_async_copy(scores_in, meta.at[pl.ds(8, 8)], load_sem.at[3])]
    for i, ref in enumerate((wg, wu, wd)):
        loads.append(pltpu.make_async_copy(ref, weights.at[i, rows_of(part)], load_sem.at[4 + i]))
    for load in loads:
        load.start()
    spread[...] = one_hot(lax.broadcasted_iota(jnp.int32, (ROWS, EXPERTS), 0) // 8
                          == lax.broadcasted_iota(jnp.int32, (ROWS, EXPERTS), 1)).astype(BF16)
    acc[...] = jnp.zeros_like(acc)
    for load in loads:
        load.wait()
    pl.semaphore_wait(entry, 49)

    remote(grad, gath_g.at[2], gath_send, gath_recv.at[2], z_back).start()
    remote(grad, gath_g.at[1], gath_send, gath_recv.at[1], z_near).start()
    for n in range(SUB):
        rows = pl.ds(n * (TOK // SUB), TOK // SUB)
        remote(tok.at[rows], ring_t.at[1, rows], ring_send, ring_recv.at[1, n], y_next).start()
        remote(tok.at[rows], ring_t.at[7, rows], ring_send, ring_recv.at[7, n], y_prev).start()
    for j, target in ((2, z_back), (1, z_near), (3, z_far)):
        remote(meta, gath_m.at[j], id_send.at[0], id_recv.at[0], target).start()

    def send_ids(dy, carry):
        target = device_at(x, lax.rem(y + dy, 8), z_pair, z_low, core)
        remote(meta.at[pl.ds(0, 8)], ring_i.at[dy], id_send.at[1], id_recv.at[1], target).start()
        return carry

    lax.fori_loop(1, 8, send_ids, 0)
    remote(own_weights, own_weights, w_send, w_recv.at[0], other_chip).start()
    remote(own_weights, own_weights, w_send, w_recv.at[1], other_core).start()

    def send_tokens(dy):
        block = tok if dy == 0 else ring_t.at[dy]
        chunk, side = place_of(dy)
        rows = pl.ds(dy * TOK, TOK)
        send_t[rows] = dot(pick_y[rows], block[...], ((1,), (0,))).astype(BF16)

        def one(index, carry):
            j, dx = lax.rem(index, 4), index // 4
            dz = jnp.where(j == 0, 0, jnp.where(j == 3, 2, jnp.where(j == 1, dz_near, dz_back)))
            z_low_to = jnp.where(j < 2, z_low, 1 - z_low)
            x_to, z_to = lax.rem(x + dx, 4), lax.rem(z_pair + dz, 4)
            src = pl.ds(pl.multiple_of(dy * TOK + (z_to * 4 + x_to) * 8, 8), 8)
            dst = pl.ds(pl.multiple_of(slot_of(chunk, side, dx, j) * 8, 8), 8)

            @pl.when(index == 0)
            def _():
                pltpu.make_async_copy(send_t.at[src], recv_t.at[dst], recv_t_sem.at[chunk]).start()

            @pl.when(index > 0)
            def _():
                target = device_at(x_to, y, z_to, z_low_to, core)
                remote(send_t.at[src], recv_t.at[dst], send_sem.at[0], recv_t_sem.at[chunk], target).start()

            return carry

        lax.fori_loop(0, 16, one, 0)

    def scale_grads(j):
        block = grad if j == 0 else gath_g.at[j]
        rows = pl.ds(j * 256, 256)
        send_g[rows] = dot(gated_z[rows], block[...], ((1,), (0,))).astype(BF16)

    def send_grads(chunk):
        def one(index, carry):
            side, j, dx = lax.rem(index, 2), lax.rem(index // 2, 4), index // 8
            dy = dy_of(chunk, side)
            x_to, y_to = lax.rem(x + dx, 4), lax.rem(y + dy, 8)
            src = pl.ds(pl.multiple_of(j * 256 + (y_to * 4 + x_to) * 8, 8), 8)
            dst = pl.ds(pl.multiple_of(slot_of(chunk, side, dx, j) * 8, 8), 8)
            here = (dx + dy) == 0

            @pl.when(here)
            def _():
                pltpu.make_async_copy(send_g.at[src], recv_g.at[dst], recv_g_sem.at[chunk]).start()

            @pl.when(jnp.logical_not(here))
            def _():
                target = device_at(x_to, y_to, z_pair, z_low, core)
                remote(send_g.at[src], recv_g.at[dst], send_sem.at[1], recv_g_sem.at[chunk], target).start()

            return carry

        lax.fori_loop(0, 32, one, 0)

    def ring_rows(n):
        return pl.ds(n * (TOK // SUB), TOK // SUB)

    def wait_ring(dy, n):
        ref = ring_t.at[dy, ring_rows(n)]
        pltpu.make_async_copy(ref, ref, ring_recv.at[dy, n]).wait()

    def pass_on(dy, to, n, target):
        remote(ring_t.at[dy, ring_rows(n)], ring_t.at[to, ring_rows(n)],
               ring_send, ring_recv.at[to, n], target).start()

    def wait_gath(j):
        pltpu.make_async_copy(gath_g.at[j], gath_g.at[j], gath_recv.at[j]).wait()

    metas = gath_m.at[pl.ds(1, 3)]
    pltpu.make_async_copy(metas, metas, id_recv.at[0]).wait()
    all_ids = ring_i.at[pl.ds(1, 7)]
    pltpu.make_async_copy(all_ids, all_ids, id_recv.at[1]).wait()
    pick_z[...], gated_z[...] = routing([meta[0:8]] + [gath_m[j, 0:8] for j in range(1, 4)],
                                        lambda e: (e // 4) * 16 + z_pair * 4 + lax.rem(e, 4),
                                        [meta[8:16]] + [gath_m[j, 8:16] for j in range(1, 4)], spread[...])
    def make_pick_y():
        pick_y[...], _ = routing([meta[0:8]] + [ring_i[dy] for dy in range(1, 8)], lambda e: y * 16 + e, None, spread[...])

    def hops(step):
        for n in range(SUB):
            wait_ring(step, n)
            if step < 3 or n < SUB // 2:
                pass_on(step, step + 1, n, y_next)
            wait_ring(8 - step, n)
            if step < 3 or n >= SUB // 2:
                pass_on(8 - step, 7 - step, n, y_prev)

    def relay():
        wait_gath(2)
        remote(gath_g.at[2], gath_g.at[3], gath_send, gath_recv.at[3], z_near).start()

    w_chip = weights.at[:, rows_of(part_chip)]

    def pass_weights():
        pltpu.make_async_copy(w_chip, w_chip, w_recv.at[0]).wait()
        remote(w_chip, w_chip, w_send, w_recv.at[2], other_core).start()

    def last_block():
        for n in range(SUB):
            wait_ring(4, n)

    def wait_weights():
        for n, p in ((1, part_core), (2, part_far)):
            ref = weights.at[:, rows_of(p)]
            pltpu.make_async_copy(ref, ref, w_recv.at[n]).wait()

    def compute(c):
        rows = pl.ds(c * CHUNK, CHUNK)
        pltpu.make_async_copy(recv_t.at[rows], recv_t.at[rows], recv_t_sem.at[c]).wait()
        pltpu.make_async_copy(recv_g.at[rows], recv_g.at[rows], recv_g_sem.at[c]).wait()
        row_in = recv_t[rows]
        scaled = recv_g[rows]
        a = dot(row_in, weights[0], ((1,), (0,)))
        b = dot(row_in, weights[1], ((1,), (0,)))
        back = dot(scaled, weights[2], ((1,), (0,)))
        sig = jax.nn.sigmoid(a)
        silu = a * sig
        hidden = (silu * b).astype(BF16)
        gate_back = (back * b * sig * (1.0 + a * (1.0 - sig))).astype(BF16)
        up_back = (back * silu).astype(BF16)
        token_part = (dot(gate_back, weights[0], ((1,), (1,)))
                      + dot(up_back, weights[1], ((1,), (1,)))).astype(BF16)
        part_y[rows] = token_part[:, :CUT]
        part_z[rows] = token_part[:, CUT:]

        def give_back(index, carry):
            side, j, dx = lax.rem(index, 2), lax.rem(index // 2, 4), index // 8
            dy = dy_of(c, side)
            dz = jnp.where(j == 0, 0, jnp.where(j == 3, 2, dz_near))
            z_low_from = jnp.where(j < 2, z_low, 1 - z_low)
            x_to, y_to, z_to = lax.rem(x + 4 - dx, 4), lax.rem(y + 8 - dy, 8), lax.rem(z_pair + 4 - dz, 4)
            src = pl.ds(pl.multiple_of(slot_of(c, side, dx, j) * 8, 8), 8)
            dst_y = ret_y.at[dy, pl.ds(pl.multiple_of((z_pair * 4 + x) * 8, 8), 8)]
            dst_z = ret_z.at[j, pl.ds(pl.multiple_of((y * 4 + x) * 8, 8), 8)]
            stays_y = (dx + j) == 0
            stays_z = (dx + dy) == 0

            @pl.when(stays_z)
            def _():
                pltpu.make_async_copy(part_z.at[src], dst_z, ret_z_sem.at[j]).start()

            @pl.when(jnp.logical_not(stays_z))
            def _():
                target = device_at(x_to, y_to, z_pair, z_low, core)
                remote(part_z.at[src], dst_z, ret_send.at[1], ret_z_sem.at[j], target).start()

            @pl.when(stays_y)
            def _():
                pltpu.make_async_copy(part_y.at[src], dst_y, ret_y_sem.at[dy]).start()

            @pl.when(jnp.logical_not(stays_y))
            def _():
                target = device_at(x_to, y, z_to, z_low_from, core)
                remote(part_y.at[src], dst_y, ret_send.at[0], ret_y_sem.at[dy], target).start()

            return carry

        lax.fori_loop(0, 32, give_back, 0)
        acc[0] += dot(row_in, gate_back, ((0,), (0,)))
        acc[1] += dot(row_in, up_back, ((0,), (0,)))
        if c == CHUNKS - 1:
            start_half(0)
            start_half(1)
        acc[2] += dot(scaled, hidden, ((0,), (0,)))
        if c == CHUNKS - 1:
            start_half(2)

    def per_token_y(dy):
        pltpu.make_async_copy(ret_y.at[dy], ret_y.at[dy], ret_y_sem.at[dy]).wait()
        return dot(pick_y[pl.ds(dy * TOK, TOK)], ret_y[dy], ((0,), (0,)))

    def per_token_z(j):
        pltpu.make_async_copy(ret_z.at[j], ret_z.at[j], ret_z_sem.at[j]).wait()
        return dot(pick_z[pl.ds(j * 256, 256)], ret_z[j], ((0,), (0,)))

    low, high = pl.ds(0, TOK // 2), pl.ds(TOK // 2, TOK // 2)

    def wait_got_y(slot, rows=None):
        ref = got_y.at[slot] if rows is None else got_y.at[slot, rows]
        pltpu.make_async_copy(ref, ref, got_y_sem.at[slot]).wait()

    def start_sum_y():
        sum_y[4] = per_token_y(4).astype(BF16)
        remote(sum_y.at[4, low], got_y.at[3, low], sum_send.at[0], got_y_sem.at[3], y_prev).start()
        remote(sum_y.at[4, high], got_y.at[5, high], sum_send.at[0], got_y_sem.at[5], y_next).start()

    def step_sum_y(dy, to, target):
        total = per_token_y(dy)
        if dy == 3:
            wait_got_y(3, low)
            half = TOK // 2
            sum_y[3, 0:half] = (total[0:half] + got_y[3, 0:half].astype(F32)).astype(BF16)
            sum_y[3, half:TOK] = total[half:TOK].astype(BF16)
        elif dy == 5:
            wait_got_y(5, high)
            half = TOK // 2
            sum_y[5, 0:half] = total[0:half].astype(BF16)
            sum_y[5, half:TOK] = (total[half:TOK] + got_y[5, half:TOK].astype(F32)).astype(BF16)
        else:
            wait_got_y(dy)
            sum_y[dy] = (total + got_y[dy].astype(F32)).astype(BF16)
        remote(sum_y.at[dy], got_y.at[to], sum_send.at[0], got_y_sem.at[to], target).start()

    def half(i):
        return remote(half_s.at[i], half_r.at[i], red_send.at[i], red_recv.at[i], other_core)

    def quarter(i):
        return remote(quarter_s.at[i], quarter_r.at[i], red_send.at[3 + i], red_recv.at[3 + i], other_chip)

    def start_half(i):
        for zl in range(2):
            half_s[i, zl] = acc[i, rows_of(zl * 2 + 1 - core)].astype(BF16)
        half(i).start()

    def wait_half(i):
        half(i).wait()

    hops(1)
    relay()
    make_pick_y()
    send_tokens(0)
    scale_grads(0)
    hops(2)
    scale_grads(2)
    send_tokens(1)
    send_tokens(7)
    wait_gath(1)
    scale_grads(1)
    hops(3)
    wait_gath(3)
    scale_grads(3)
    send_grads(0)
    send_tokens(3)
    send_tokens(5)
    last_block()
    send_tokens(4)
    send_grads(1)
    send_tokens(2)
    send_tokens(6)
    send_grads(2)
    pass_weights()
    wait_weights()
    compute(0)
    send_grads(3)
    compute(1)
    start_sum_y()
    compute(2)
    step_sum_y(3, 2, y_prev)
    step_sum_y(5, 6, y_next)
    compute(3)
    for i in range(3):
        wait_half(i)
        quarter_s[i] = (acc[i, rows_of(part_chip)] + half_r[i, 1 - z_low].astype(F32)).astype(BF16)
        quarter(i).start()
    step_sum_y(2, 1, y_prev)
    step_sum_y(6, 7, y_next)
    sum_z[3] = per_token_z(3).astype(BF16)
    remote(sum_z.at[3], got_z.at[3], sum_send.at[1], got_z_sem.at[3], z_from).start()
    step_sum_y(1, 0, y_prev)
    step_sum_y(7, 4, y_next)
    sum_z[1] = per_token_z(1).astype(BF16)
    remote(sum_z.at[1], got_z.at[1], sum_send.at[1], got_z_sem.at[1], z_from).start()
    own_z2 = per_token_z(2)
    pltpu.make_async_copy(got_z.at[3], got_z.at[3], got_z_sem.at[3]).wait()
    sum_z[2] = (own_z2 + got_z[3].astype(F32)).astype(BF16)
    remote(sum_z.at[2], got_z.at[2], sum_send.at[1], got_z_sem.at[2], z_back).start()
    own_y = per_token_y(0)
    own_z = per_token_z(0)
    wait_got_y(0)
    wait_got_y(4)
    d_tok[:, 0:CUT] = (own_y + got_y[0].astype(F32) + got_y[4].astype(F32)).astype(BF16)
    for i in range(3):
        quarter(i).wait()
    outs = (g_gate, g_up, g_down)
    for i in range(3):
        outs[i][...] = acc[i, rows_of(part)] + half_r[i, z_low].astype(F32) + quarter_r[i].astype(F32)
    pltpu.make_async_copy(got_z.at[1], got_z.at[1], got_z_sem.at[1]).wait()
    pltpu.make_async_copy(got_z.at[2], got_z.at[2], got_z_sem.at[2]).wait()
    d_tok[:, CUT:D] = (own_z + got_z[1].astype(F32) + got_z[2].astype(F32)).astype(BF16)

    def wait_sent(ref, sem):
        pltpu.make_async_copy(ref, ref, sem).wait()

    wait_sent(send_t.at[pl.ds(0, ROWS - 64)], send_sem.at[0])
    wait_sent(send_g.at[pl.ds(0, ROWS - 32)], send_sem.at[1])
    wait_sent(part_y.at[pl.ds(0, ROWS - 64)], ret_send.at[0])
    wait_sent(part_z.at[pl.ds(0, ROWS - 32)], ret_send.at[1])
    wait_sent(ring_t.at[pl.ds(1, 7)], ring_send)
    wait_sent(gath_g.at[pl.ds(1, 3)], gath_send)
    wait_sent(metas, id_send.at[0])
    wait_sent(all_ids, id_send.at[1])
    wait_sent(sum_y.at[pl.ds(1, 7)], sum_send.at[0])
    wait_sent(sum_z.at[pl.ds(1, 3)], sum_send.at[1])
    for _ in range(3):
        wait_sent(w_chip, w_send)


def per_device(tokens, out_grad, expert_ids, gate_scores, w_gate, w_up, w_down):
    vmem = pl.BlockSpec(memory_space=pltpu.VMEM)
    block = jax.ShapeDtypeStruct((DQ, HID), F32)
    dma = pltpu.SemaphoreType.DMA
    operands = [pltpu.with_memory_space_constraint(value, pltpu.HBM) for value in (
        tokens, out_grad, expert_ids.T, gate_scores.T, w_gate[0], w_up[0], w_down[0])]
    d_tokens, gate, up, down = pl.pallas_call(
        body,
        out_shape=(jax.ShapeDtypeStruct((TOK, D), BF16), block, block, block),
        in_specs=[pl.BlockSpec(memory_space=pl.ANY)] * 7,
        out_specs=(vmem,) * 4,
        scratch_shapes=[
            pltpu.VMEM((TOK, D), BF16),
            pltpu.VMEM((TOK, D), BF16),
            pltpu.VMEM((16, TOK), jnp.int32),
            pltpu.VMEM((ROWS, EXPERTS), BF16),
            pltpu.VMEM((ROWS, TOK), BF16),
            pltpu.VMEM((ROWS, TOK), BF16),
            pltpu.VMEM((ROWS, TOK), BF16),
            pltpu.VMEM((8, TOK, D), BF16),
            pltpu.VMEM((8, 8, TOK), jnp.int32),
            pltpu.VMEM((4, TOK, D), BF16),
            pltpu.VMEM((4, 16, TOK), jnp.int32),
            pltpu.VMEM((ROWS, D), BF16),
            pltpu.VMEM((ROWS, D), BF16),
            pltpu.VMEM((ROWS, D), BF16),
            pltpu.VMEM((ROWS, D), BF16),
            pltpu.VMEM((ROWS, CUT), BF16),
            pltpu.VMEM((ROWS, D - CUT), BF16),
            pltpu.VMEM((8, TOK, CUT), BF16),
            pltpu.VMEM((4, 256, D - CUT), BF16),
            pltpu.VMEM((8, TOK, CUT), BF16),
            pltpu.VMEM((4, TOK, D - CUT), BF16),
            pltpu.VMEM((8, TOK, CUT), BF16),
            pltpu.VMEM((4, TOK, D - CUT), BF16),
            pltpu.VMEM((3, D, HID), BF16),
            pltpu.VMEM((3, D, HID), F32),
            pltpu.VMEM((3, 2, DQ, HID), BF16),
            pltpu.VMEM((3, 2, DQ, HID), BF16),
            pltpu.VMEM((3, DQ, HID), BF16),
            pltpu.VMEM((3, DQ, HID), BF16),
            dma((7,)),
            dma,
            dma((8, SUB)),
            dma,
            dma((4,)),
            dma((2,)),
            dma((2,)),
            dma((2,)),
            dma((CHUNKS,)),
            dma((CHUNKS,)),
            dma,
            dma((3,)),
            dma((2,)),
            dma((8,)),
            dma((4,)),
            dma((2,)),
            dma((8,)),
            dma((4,)),
            dma((6,)),
            dma((6,)),
        ],
        compiler_params=pltpu.CompilerParams(
            collective_id=0, has_side_effects=True, vmem_limit_bytes=40 << 20),
        name="expert_layer_backward",
    )(*operands)
    return d_tokens, gate[None], up[None], down[None]


def solution(mesh):
    rows = P(("expert", "dp"), None)
    blocks = P(("expert", "dp"), None, None)
    return jax.shard_map(
        per_device,
        mesh=mesh,
        in_specs=(rows, rows, rows, rows, blocks, blocks, blocks),
        out_specs=(rows, blocks, blocks, blocks),
        check_vma=False,
    )
```
